512 devices in a mesh: dp: 128 (over z_hi, y, x, core), tm: 4 (over z_lo).
Axes of the slice: x: 4, y: 4, z: 16 (z_hi: 4, z_lo: 4; z = z_hi * 4 + z_lo), core: 2. Of those that a mesh axis runs over, the one named last changes fastest.
Arguments:
- feats: bfloat16 [393216, 512], P(('dp', 'tm')), may hold values from -40 to 40, as said below
- codes: int32 [128, 2, 1536], P('dp', None, 'tm'), may hold values from 0 to 1023, as said below
- conv_weight: bfloat16 [2048, 512], replicated, may hold values from -0.125 to 0.125
- conv_bias: float32 [512], replicated, may hold values from -3 to 3
- proj_weight: bfloat16 [512, 256], replicated, may hold values from -0.25 to 0.25
- codebooks: bfloat16 [2, 1024, 256], replicated, may hold values from -4.1875 to 4.1875
Outputs:
- feat_grad: bfloat16 [393216, 512], P(('dp', 'tm'))
- conv_grad: float32 [2048, 512], P(('dp', 'tm'))
- bias_grad: float32 [512], replicated
- proj_grad: float32 [512, 256], replicated
- code_means: bfloat16 [2, 1024, 256], P(None, 'tm')
- code_usage: float32 [2, 1024], P(None, 'tm')
The draws below stay inside these ranges and needn't reach their ends.
Inputs may be any that keep to these rules, and one draw needn't show every extreme that they name: `feats`: each clip has its own overall scale, and rows vary in scale within a clip. Codes are used with strongly unequal frequencies; on every level some codes occur in no frame.
All inputs are finite; a program needn't handle non-finite values.
Results may differ from the reference program's by a relative error of at most 0.0075.
Values may be sent and summed in bfloat16 or wider, within the bound.
A program may use at most 64 MiB of HBM per device.

```python
import jax
import jax.numpy as jnp
from jax import lax

D = 512
DZ = 256
CODES = 1024
KW = 4
LEVELS = 2
CLIPS = 128
FRAMES = 1536
TOTAL = 196608
ROWS_IN = 393216


def draw_feats(key, part):
    key_base, key_clip, key_row = jax.random.split(jax.random.fold_in(key, 11), 3)
    row_total = CLIPS * 2 * FRAMES
    base = jax.random.normal(key_base, (row_total, D), jnp.float32)
    base = jnp.clip(base, -6.0, 6.0)
    clip_scale = jnp.exp(jax.random.uniform(key_clip, (CLIPS, 1), jnp.float32, 0.0, jnp.log(3.0)))
    row_scale = jnp.exp(jax.random.uniform(key_row, (row_total, 1), jnp.float32, -0.69, 0.69))
    scale = jnp.repeat(clip_scale, 2 * FRAMES, axis=0) * row_scale
    return (base * scale).astype(jnp.bfloat16)


def move_to(ranking, value, place):
    current = jnp.argmax(ranking == value).astype(jnp.int32)
    displaced = ranking[place]
    ranking = ranking.at[current].set(displaced)
    return ranking.at[place].set(value)


def draw_codes(key, part):
    living = CODES - CODES // 16
    key_order, key_ceiling, key_rank, key_place = jax.random.split(jax.random.fold_in(key, 23), 4)
    columns = []
    for level_index in range(LEVELS):
        ranking = jax.random.permutation(jax.random.fold_in(key_order, level_index), CODES).astype(jnp.int32)
        places = jax.random.randint(jax.random.fold_in(key_place, level_index), (2,), 0, living // 4).astype(jnp.int32)
        ranking = move_to(ranking, 0, places[0])
        ranking = move_to(ranking, CODES - 1, places[1] + living // 4)
        ceiling = jax.random.randint(jax.random.fold_in(key_ceiling, level_index), (CLIPS, FRAMES), 1, living + 1)
        rank_index = jax.random.randint(jax.random.fold_in(key_rank, level_index), (CLIPS, FRAMES), 0, ceiling)
        columns.append(ranking[rank_index])
    return jnp.stack(columns, 1).astype(jnp.int32)


def noise(stream_key, dims, width, bound, held_as=jnp.bfloat16):
    drawn = jax.random.normal(stream_key, dims, jnp.float32) * width
    return jnp.minimum(jnp.maximum(drawn, -bound), bound).astype(held_as)


def setup_inputs(seed: int = 0) -> dict:
    arg_keys = jax.random.split(jax.random.key(seed), 7)
    return {
        "feats": draw_feats(jax.random.fold_in(arg_keys[6], 71), 0),
        "codes": draw_codes(jax.random.fold_in(arg_keys[6], 71), 0),
        "conv_weight": noise(arg_keys[2], (KW * D, D), (KW * D) ** -0.5, 0.125),
        "conv_bias": noise(arg_keys[3], (D,), 0.5, 3.0, jnp.float32),
        "proj_weight": noise(arg_keys[4], (D, DZ), D ** -0.5, 0.25),
        "codebooks": noise(arg_keys[5], (LEVELS, CODES, DZ), 0.7, 4.1875),
    }


def clip_terms(running, inputs, conv_weight, conv_bias, proj_weight, codebooks):
    clip_feats, clip_codes = inputs
    frame_count = clip_feats.shape[0] // 2
    channels = clip_feats.shape[1]
    padded = jnp.concatenate([jnp.zeros((2, channels), clip_feats.dtype), clip_feats], 0)
    paired = padded.reshape(frame_count + 1, 2 * channels)
    unfold = jnp.concatenate([paired[:-1], paired[1:]], 1)
    conv_out = jnp.dot(unfold, conv_weight, preferred_element_type=jnp.float32) + conv_bias
    hidden = conv_out.astype(jnp.bfloat16)
    latent = jnp.dot(hidden, proj_weight, preferred_element_type=jnp.float32)
    residual = latent
    grad_total = jnp.zeros(latent.shape, jnp.float32)
    sums_list = []
    counts_list = []
    code_ids = jnp.arange(CODES, dtype=jnp.int32)
    for level_index in range(LEVELS):
        matches = clip_codes[level_index][:, None] == code_ids[None, :]
        onehot = matches.astype(jnp.float32)
        sums_list.append(jnp.dot(onehot.T, residual, precision=lax.Precision.HIGHEST))
        counts_list.append(jnp.sum(onehot, 0))
        chosen = jnp.dot(matches.astype(jnp.bfloat16), codebooks[level_index], preferred_element_type=jnp.float32)
        residual = residual - chosen
        grad_total = grad_total + residual
    latent_grad = grad_total.astype(jnp.bfloat16)
    proj_term = jnp.dot(hidden.T, latent_grad, preferred_element_type=jnp.float32)
    hidden_grad = jnp.dot(latent_grad, proj_weight.T, preferred_element_type=jnp.float32).astype(jnp.bfloat16)
    bias_term = jnp.sum(hidden_grad.astype(jnp.float32), 0)
    corr_term = jnp.dot(unfold.T, latent_grad, preferred_element_type=jnp.float32)
    grad_unfold = jnp.dot(hidden_grad, conv_weight.T, preferred_element_type=jnp.float32)
    first_half = grad_unfold[:, :2 * channels]
    second_half = grad_unfold[:, 2 * channels:]
    shifted = jnp.concatenate([first_half[1:], jnp.zeros((1, 2 * channels), jnp.float32)], 0)
    grad_paired = shifted + second_half
    grad_feats = grad_paired.reshape(2 * frame_count, channels).astype(jnp.bfloat16)
    corr_sum, proj_sum, bias_sum, code_sums, code_counts = running
    updated = (corr_sum + corr_term, proj_sum + proj_term, bias_sum + bias_term,
               code_sums + jnp.stack(sums_list), code_counts + jnp.stack(counts_list))
    return updated, grad_feats


def reference(feats, codes, conv_weight, conv_bias, proj_weight, codebooks):
    clip_rows = feats.reshape(CLIPS, 2 * FRAMES, D)
    init = (jnp.zeros((KW * D, DZ), jnp.float32), jnp.zeros((D, DZ), jnp.float32),
            jnp.zeros((D,), jnp.float32), jnp.zeros((LEVELS, CODES, DZ), jnp.float32),
            jnp.zeros((LEVELS, CODES), jnp.float32))

    def step_clip(running, inputs):
        return clip_terms(running, inputs, conv_weight, conv_bias, proj_weight, codebooks)

    running, grads = lax.scan(step_clip, init, (clip_rows, codes))
    corr_sum, proj_sum, bias_sum, code_sums, code_counts = running
    conv_grad = jnp.dot(corr_sum, proj_weight.astype(jnp.float32).T, precision=lax.Precision.HIGHEST) / TOTAL
    proj_grad = proj_sum / TOTAL
    bias_grad = bias_sum / TOTAL
    code_means = (code_sums / jnp.maximum(code_counts, 1.0)[:, :, None]).astype(jnp.bfloat16)
    code_usage = code_counts * (CODES / TOTAL)
    return grads.reshape(ROWS_IN, D), conv_grad, bias_grad, proj_grad, code_means, code_usage
```

```python
import functools

import jax
import jax.numpy as jnp
from jax import lax
from jax.experimental import pallas as pl
from jax.experimental.pallas import tpu as pltpu
from jax.sharding import PartitionSpec as P

MESH = pl.DeviceIdType.MESH
BF = jnp.bfloat16
F32 = jnp.float32
NC = 2


def dot(a, b, ca=1, cb=0):
    return lax.dot_general(a, b, (((ca,), (cb,)), ((), ())), preferred_element_type=F32)


class Sems:
    def __init__(self, send, recv):
        self.send, self.recv, self.count, self.started, self.index = send, recv, 0, [], {}

    def copy(self, src, dst, device):
        index = self.count
        self.count += 1
        made = pltpu.make_async_remote_copy(
            src_ref=src, dst_ref=dst, send_sem=self.send.at[index], recv_sem=self.recv.at[index],
            device_id=device, device_id_type=MESH,
        )
        self.index[id(made)] = index
        return made

    def arrived(self, made, ref, device):
        index = self.index[id(made)]
        pltpu.make_async_remote_copy(
            src_ref=ref, dst_ref=ref, send_sem=self.send.at[index], recv_sem=self.recv.at[index],
            device_id=device, device_id_type=MESH,
        ).wait_recv()

    def start(self, src, dst, device):
        made = self.copy(src, dst, device)
        made.start()
        self.started.append(made)
        return made


def kernel(g, feats, codes, conv_w, conv_b, proj_w, books,
           fg_out, conv_out, bias_out, proj_out, means_out, usage_out,
           feats_v, cw_v, pw_v, books_v, fx, unf, acc_v, hid, lat, lg_v, hgf, halo_v, next_v, fg_f, fg_v,
           s0_0, s0_c, s0_1, s0_r1, s0_2, s0_r2,
           s1_0, s1_c, s1_1, s1_r1, s1_2, s1_r2,
           pr_0, pr_c, pr_1, pr_r1, pr_2, pr_r2,
           ca_0, ca_c, ca_1, ca_r1, ca_2, ca_r2,
           cb_0, cb_c, cb_1, cb_r1, cb_2, cb_r2,
           sm_c, sm_x, sm_y, sm_l, sm_h, sm_f,
           zl_s, zl_r, zh_r, ch_s, ch_r, cl_r, conv_f, ag_s, ag_p,
           in_sem, out_sem, send_sem, recv_sem):
    nx, ny, zh_n, zl_n = g["nx"], g["ny"], g["zh"], g["zl"]
    frames, chan, dz, book = g["frames"], g["chan"], g["dz"], g["book"]
    total = g["total"]
    rs, rp, rpd = g["rs"], g["rp"], g["rpd"]
    tile = zl_n * rpd
    zhh = zh_n // 2
    lanes = chan // 128

    dp, zl = lax.axis_index("dp"), lax.axis_index("tm")
    c = dp % NC
    x = dp // NC % nx
    y = dp // (NC * nx) % ny
    zh = dp // (NC * nx * ny)

    def dev(c_, x_, y_, zh_, zl_):
        return (((zh_ * ny + y_) * nx + x_) * NC + c_, zl_)

    def at_core():
        return dev(1 - c, x, y, zh, zl)

    def at_x(d):
        return dev(c, (x + d) % nx, y, zh, zl)

    def at_y(d):
        return dev(c, x, (y + d) % ny, zh, zl)

    def at_l(d):
        return dev(c, x, y, zh, (zl + d) % zl_n)

    def at_h(d):
        return dev(c, x, y, (zh + d) % zh_n, zl)

    sems = Sems(send_sem, recv_sem)

    barrier = pltpu.get_barrier_semaphore()
    partners = [at_core()]
    for ring, n in ((at_x, nx), (at_y, ny), (at_l, zl_n), (at_h, zh_n)):
        partners += [ring(d) for d in range(1, n)]
    for partner in partners:
        pl.semaphore_signal(barrier, inc=1, device_id=partner, device_id_type=MESH)

    half = 2 * chan
    loads = [
        pltpu.make_async_copy(feats, feats_v, in_sem.at[0]),
        pltpu.make_async_copy(conv_w.at[pl.ds(half, half)], cw_v.at[pl.ds(half, half)], in_sem.at[1]),
        pltpu.make_async_copy(conv_w.at[pl.ds(0, half)], cw_v.at[pl.ds(0, half)], in_sem.at[2]),
        pltpu.make_async_copy(proj_w, pw_v, in_sem.at[3]),
        pltpu.make_async_copy(books, books_v, in_sem.at[4]),
    ]
    for load in loads:
        load.start()

    rows_in = 2 * frames
    loads[0].wait()
    for k in range(lanes):
        fx[k, pl.ds(8, rows_in), :] = feats_v[:, k * 128:(k + 1) * 128].astype(F32)

    def spread(start, tap):
        for k in range(lanes):
            piece = fx[k, pl.ds(start, frames, stride=2), :]
            unf[:, tap * chan + k * 128:tap * chan + (k + 1) * 128] = piece.astype(BF)

    spread(8, 2)
    spread(9, 3)
    loads[1].wait()
    acc_v[...] = dot(unf[:, half:], cw_v[half:, :])

    pl.semaphore_wait(barrier, len(partners))
    halo = sems.copy(feats_v.at[pl.ds(rows_in - 16, 16)], halo_v, at_l(1))

    @pl.when(zl < zl_n - 1)
    def _():
        halo.start()

    code_rows = codes[0].astype(F32)
    lane_ids = lax.broadcasted_iota(jnp.int32, (frames, book), 1).astype(F32)

    def onehot(level):
        eye = (lax.broadcasted_iota(jnp.int32, (frames, frames), 0)
               == lax.broadcasted_iota(jnp.int32, (frames, frames), 1))
        column = jnp.sum(jnp.where(eye, code_rows[level:level + 1, :], 0.0), 1, keepdims=True)
        return (column == lane_ids).astype(F32)

    per_q = book // zl_n
    per_c = nx * ny * rs

    def onehot_t(level, side):
        rows = nx * ny * zl_n * rs
        p = lax.broadcasted_iota(jnp.int32, (rows, 1), 0)
        i = p % rs
        q = p // rs % zl_n
        if level == 0:
            yy = p // (rs * zl_n) % ny
            xx = p // (rs * zl_n * ny)
        else:
            xx = p // (rs * zl_n) % nx
            yy = p // (rs * zl_n * nx)
        ids = q * per_q + side * per_c + (xx * ny + yy) * rs + i
        return (ids.astype(F32) == code_rows[level:level + 1, :]).astype(F32).astype(BF)

    small_rows = book // 128
    oh0 = onehot(0)
    oh1 = onehot(1)
    for level, oh in enumerate((oh0, oh1)):
        count = jnp.sum(oh, 0, keepdims=True)
        for r in range(small_rows):
            sm_c[0, pl.ds(level * small_rows + r, 1), :] = count[:, r * 128:(r + 1) * 128]

    @pl.when(zl == 0)
    def _():
        halo_v[...] = jnp.zeros(halo_v.shape, BF)

    @pl.when(zl > 0)
    def _():
        halo.wait_recv()

    last = halo_v[...].astype(F32)[8:16, :]
    for k in range(lanes):
        fx[k, pl.ds(0, 8), :] = last[:, k * 128:(k + 1) * 128]
    spread(6, 0)
    spread(7, 1)
    loads[2].wait()
    conv = acc_v[...] + dot(unf[:, :half], cw_v[:half, :])
    hid[...] = (conv + conv_b[...]).astype(BF)
    loads[3].wait()
    lat[...] = dot(hid[...], pw_v[...])

    def level_sums(level, ref0, refc):
        value = lat[...]
        hi = value.astype(BF)
        lo = (value - hi.astype(F32)).astype(BF)

        def part(side):
            oh = onehot_t(level, side)
            made = dot(oh, hi) + dot(oh, lo)
            ref0[side] = made.astype(BF).reshape(ref0.shape[1:])

        part(1 - c)
        copy = sems.start(ref0.at[1 - c], refc, at_core())
        part(c)
        return copy

    s0_core = level_sums(0, s0_0, s0_c)
    loads[4].wait()
    r1 = lat[...] - dot(oh0.astype(BF), books_v[0])
    lat[...] = r1
    s1_core = level_sums(1, s1_0, s1_c)

    def stage1(core_copy, ref0, refc, ref1, refr, ring, n, me):
        core_copy.wait_recv()
        ref1[...] = (ref0[c].astype(F32) + refc[...].astype(F32)).astype(BF)
        return [sems.start(ref1.at[(me + d) % n], refr.at[d - 1], ring(d)) for d in range(1, n)]

    def stage2(copies, ref1, refr, ref2, refr2, ring, n, me, me1):
        made = ref1[me1].astype(F32)
        for d, copy in enumerate(copies):
            copy.wait_recv()
            made = made + refr[d].astype(F32)
        ref2[...] = made.astype(BF).reshape(ref2.shape)
        return [sems.start(ref2.at[(me + d) % n], refr2.at[d - 1], ring(d)) for d in range(1, n)]

    def finish(copies, ref2, refr2, me):
        made = ref2[me].astype(F32)
        for d, copy in enumerate(copies):
            copy.wait_recv()
            made = made + refr2[d].astype(F32)
        return made

    s0_x = stage1(s0_core, s0_0, s0_c, s0_1, s0_r1, at_x, nx, x)

    value = lat[...]
    lg = (value + (value - dot(oh1.astype(BF), books_v[1]))).astype(BF)
    lg_v[...] = lg
    pr_0[...] = dot(hid[...], lg, 0, 0).astype(BF).reshape(pr_0.shape)
    pr_core = sems.start(pr_0.at[1 - c], pr_c, at_core())

    s1_y = stage1(s1_core, s1_0, s1_c, s1_1, s1_r1, at_y, ny, y)

    hg = dot(lg, pw_v[...], 1, 1).astype(BF)
    hid[...] = hg
    hgw = hg.astype(F32)
    hgf[pl.ds(0, frames), :] = hgw
    nxt = sems.copy(hid.at[pl.ds(0, 16)], next_v, at_l(-1 + zl_n))

    @pl.when(zl > 0)
    def _():
        nxt.start()

    bias = jnp.sum(hgw, 0, keepdims=True)
    for r in range(lanes):
        sm_c[0, pl.ds(2 * small_rows + r, 1), :] = bias[:, r * 128:(r + 1) * 128]
    pad = sm_c.shape[1] - 2 * small_rows - lanes
    if pad:
        sm_c[0, pl.ds(2 * small_rows + lanes, pad), :] = jnp.zeros((pad, 128), F32)
    sm_core = sems.start(sm_c.at[0], sm_c.at[1], at_core())

    def corr(base, ref0, x_first):
        group = nx * NC * tile
        for zz in range(zhh):
            for yy in range(ny):
                start = base + (zz * ny + yy) * group
                made = dot(unf[:, start:start + group], lg_v[...], 0, 0).astype(BF)
                for xx in range(nx):
                    for cc in range(NC):
                        at = (xx * NC + cc) * tile
                        a, b = (xx, yy) if x_first else (yy, xx)
                        row = (b * zhh + zz) * tile
                        ref0[cc, a, row:row + tile, :] = made[at:at + tile, :]

    corr(0, ca_0, True)
    ca_core = sems.start(ca_0.at[1 - c], ca_c, at_core())
    pr_x = stage1(pr_core, pr_0, pr_c, pr_1, pr_r1, at_x, nx, x)
    corr(half, cb_0, False)
    cb_core = sems.start(cb_0.at[1 - c], cb_c, at_core())

    def small(copies, ref, me, n, nxt_ref):
        for copy in copies:
            copy.wait_recv()
        made = None
        for j in range(n):
            piece = ref[(me - j + n) % n]
            made = piece if made is None else made + piece
        nxt_ref[...] = made

    def small_send(ref, ring, n):
        return [sems.start(ref.at[0], ref.at[d], ring(d)) for d in range(1, n)]

    small([sm_core], sm_c, c, NC, sm_x.at[0])
    sm_xs = small_send(sm_x, at_x, nx)

    s0_y = stage2(s0_x, s0_1, s0_r1, s0_2, s0_r2, at_y, ny, y, x)
    s1_x = stage2(s1_y, s1_1, s1_r1, s1_2, s1_r2, at_x, nx, x, y)
    pr_y = stage2(pr_x, pr_1, pr_r1, pr_2, pr_r2, at_y, ny, y, x)
    small(sm_xs, sm_x, x, nx, sm_y.at[0])
    sm_ys = small_send(sm_y, at_y, ny)
    ca_x = stage1(ca_core, ca_0, ca_c, ca_1, ca_r1, at_x, nx, x)
    cb_y = stage1(cb_core, cb_0, cb_c, cb_1, cb_r1, at_y, ny, y)

    s0_d = finish(s0_y, s0_2, s0_r2, y)
    s1_d = finish(s1_x, s1_2, s1_r2, x)
    pr_d = finish(pr_y, pr_2, pr_r2, y)
    for q in range(zl_n):
        zl_s[q] = jnp.concatenate(
            [s0_d[q * rs:(q + 1) * rs], s1_d[q * rs:(q + 1) * rs], pr_d], 0).astype(BF)
    zl_c = [sems.start(zl_s.at[(zl + d) % zl_n], zl_r.at[d], at_l(d)) for d in range(1, zl_n)]
    zl_r[0] = zl_s[zl]
    small(sm_ys, sm_y, y, ny, sm_l.at[0])
    sm_ls = small_send(sm_l, at_l, zl_n)

    @pl.when(zl == zl_n - 1)
    def _():
        next_v[...] = jnp.zeros(next_v.shape, BF)

    @pl.when(zl < zl_n - 1)
    def _():
        nxt.wait_recv()

    hgf[pl.ds(frames, 8), :] = next_v[...].astype(F32)[0:8, :]
    lg_next = hgf[pl.ds(1, frames), :].astype(BF)

    def feat_part(part):
        made = (dot(lg_next, cw_v[pl.ds(part * chan, chan), :], 1, 1)
                + dot(hid[...], cw_v[pl.ds(half + part * chan, chan), :], 1, 1))
        for k in range(lanes):
            fg_f[k, pl.ds(part, frames, stride=2), :] = made[:, k * 128:(k + 1) * 128]

    feat_part(0)
    feat_part(1)

    def summed(copies, ref, me, n):
        for copy in copies:
            copy.wait_recv()
        made = None
        for j in range(n):
            piece = ref[(me - j + n) % n].astype(F32)
            made = piece if made is None else made + piece
        return made

    zh_r[0] = summed(zl_c, zl_r, zl, zl_n).astype(BF)
    zh_c = [sems.start(zh_r.at[0], zh_r.at[d], at_h(d)) for d in range(1, zh_n)]
    small(sm_ls, sm_l, zl, zl_n, sm_h.at[0])
    sm_hs = small_send(sm_h, at_h, zh_n)

    ca_y = stage2(ca_x, ca_1, ca_r1, ca_2, ca_r2, at_y, ny, y, x)
    cb_x = stage2(cb_y, cb_1, cb_r1, cb_2, cb_r2, at_x, nx, x, y)

    for k in range(lanes):
        fg_v[:, k * 128:(k + 1) * 128] = fg_f[k].astype(BF)
    fg_store = pltpu.make_async_copy(fg_v, fg_out, out_sem.at[0])
    fg_store.start()

    ca_d = finish(ca_y, ca_2, ca_r2, y)
    cb_d = finish(cb_x, cb_2, cb_r2, x)
    for zz in range(zhh):
        ch_s[zz] = ca_d[zz * tile:(zz + 1) * tile].astype(BF)
        ch_s[zhh + zz] = cb_d[zz * tile:(zz + 1) * tile].astype(BF)
    ch_c = [sems.start(ch_s.at[(zh + d) % zh_n], ch_r.at[d], at_h(d)) for d in range(1, zh_n)]
    ch_r[0] = ch_s[zh]

    small(sm_hs, sm_h, zh, zh_n, sm_f)
    q_rows = per_q // 128
    base = c * per_c + (x * ny + y) * rs
    ids = lax.broadcasted_iota(jnp.int32, (rs, 128), 1) - lax.broadcasted_iota(jnp.int32, (rs, 128), 0)
    columns = []
    for level in range(2):
        row = sm_f[pl.ds(level * small_rows + zl * q_rows + base // 128, 1), :]
        columns.append(jnp.sum(jnp.where(ids == base % 128, row, 0.0), 1, keepdims=True))
        for r in range(q_rows):
            count = sm_f[pl.ds(level * small_rows + zl * q_rows + r, 1), :]
            usage_out[level:level + 1, r * 128:(r + 1) * 128] = count * (book / total)
    for r in range(lanes):
        bias_out[:, r * 128:(r + 1) * 128] = sm_f[2 * small_rows + r:2 * small_rows + r + 1, :] / total
    counts = jnp.maximum(jnp.concatenate(columns, 0), 1.0)

    done = summed(zh_c, zh_r, zh, zh_n)
    ag_s[c, x, y] = (done[:2 * rs] / counts).astype(BF)
    ag_p[c, y, x] = done[2 * rs:].astype(BF)
    gs = [sems.start(ag_s.at[c, x, y], ag_s.at[c, x, y], at_y(d)) for d in range(1, ny)]
    gp = [sems.start(ag_p.at[c, y, x], ag_p.at[c, y, x], at_x(d)) for d in range(1, nx)]

    def gathered(sem_copies, ref_of, n, me):
        for d, copy in enumerate(sem_copies):
            src = (me - (d + 1) + n) % n
            sems.arrived(copy, ref_of(src), at_core())

    gathered(gs, lambda j: ag_s.at[c, x, j], ny, y)
    gs2 = [sems.start(ag_s.at[c, x], ag_s.at[c, x], at_x(d)) for d in range(1, nx)]
    gathered(gp, lambda j: ag_p.at[c, y, j], nx, x)
    gp2 = [sems.start(ag_p.at[c, y], ag_p.at[c, y], at_y(d)) for d in range(1, ny)]

    cl_r[0] = summed(ch_c, ch_r, zh, zh_n).astype(BF)
    cl_c = [sems.start(cl_r.at[0], cl_r.at[d], at_l(d)) for d in range(1, zl_n)]

    gathered(gs2, lambda j: ag_s.at[c, j], nx, x)
    gs3 = sems.start(ag_s.at[c], ag_s.at[c], at_core())
    gathered(gp2, lambda j: ag_p.at[c, j], ny, y)
    gp3 = sems.start(ag_p.at[c], ag_p.at[c], at_core())

    owned = summed(cl_c, cl_r, zl, zl_n)
    top = owned.astype(BF)
    low = (owned - top.astype(F32)).astype(BF)
    made = (dot(top, pw_v[...], 1, 1) + dot(low, pw_v[...], 1, 1)) / total
    conv_f[...] = made
    picked = None
    for q in range(zl_n):
        piece = jnp.where(zl == q, conv_f[q * rpd:(q + 1) * rpd, :], 0.0)
        picked = piece if picked is None else picked + piece
    conv_out[...] = picked

    gathered([gs3], lambda j: ag_s.at[1 - c], 1, 0)
    for cc in range(NC):
        for xx in range(nx):
            for level in range(2):
                rows = [ag_s[cc, xx, yy].astype(F32)[level * rs:(level + 1) * rs] for yy in range(ny)]
                at = cc * per_c + xx * ny * rs
                means_out[level, at:at + ny * rs, :] = jnp.concatenate(rows, 0).astype(BF)
    gathered([gp3], lambda j: ag_p.at[1 - c], 1, 0)
    for cc in range(NC):
        for xx in range(nx):
            for yy in range(ny):
                at = ((cc * nx + xx) * ny + yy) * rp
                proj_out[at:at + rp, :] = ag_p[cc, yy, xx].astype(F32) * (1.0 / total)

    fg_store.wait()
    for copy in sems.started:
        copy.wait_send()

    @pl.when(zl < zl_n - 1)
    def _():
        halo.wait_send()

    @pl.when(zl > 0)
    def _():
        nxt.wait_send()


def shards(g, feats, codes, conv_weight, conv_bias, proj_weight, codebooks):
    rows_in, chan = feats.shape
    frames = rows_in // 2
    dz = proj_weight.shape[1]
    book = codebooks.shape[1]
    nx, ny, zhn, zln = g["nx"], g["ny"], g["zh"], g["zl"]
    devices = NC * nx * ny * zhn * zln
    taps = conv_weight.shape[0]
    g = dict(g, frames=frames, chan=chan, dz=dz, book=book, total=float(frames * devices),
             rs=book // (NC * nx * ny * zln), rp=chan // (NC * nx * ny), rpd=taps // devices)
    rs, rp, rpd = g["rs"], g["rp"], g["rpd"]
    tile = zln * rpd
    lanes = chan // 128

    def flow(a, b, rows):
        return [
            pltpu.VMEM((NC, a, b * rows, dz), BF),
            pltpu.VMEM((a, b * rows, dz), BF),
            pltpu.VMEM((a, b * rows, dz), BF),
            pltpu.VMEM((max(a - 1, 1), b * rows, dz), BF),
            pltpu.VMEM((b, rows, dz), BF),
            pltpu.VMEM((max(b - 1, 1), rows, dz), BF),
        ]

    small = -(-(2 * book // 128 + lanes) // 8) * 8
    zrows = 2 * rs + rp
    scratch = [
        pltpu.VMEM((rows_in, chan), BF),
        pltpu.VMEM((taps, chan), BF),
        pltpu.VMEM((chan, dz), BF),
        pltpu.VMEM((2, book, dz), BF),
        pltpu.VMEM((lanes, rows_in + 8, 128), F32),
        pltpu.VMEM((frames, taps), BF),
        pltpu.VMEM((frames, chan), F32),
        pltpu.VMEM((frames, chan), BF),
        pltpu.VMEM((frames, dz), F32),
        pltpu.VMEM((frames, dz), BF),
        pltpu.VMEM((frames + 8, chan), F32),
        pltpu.VMEM((16, chan), BF),
        pltpu.VMEM((16, chan), BF),
        pltpu.VMEM((lanes, rows_in, 128), F32),
        pltpu.VMEM((rows_in, chan), BF),
    ]
    scratch += flow(nx, ny, zln * rs)
    scratch += flow(ny, nx, zln * rs)
    scratch += flow(nx, ny, rp)
    scratch += flow(nx, ny, zhn // 2 * tile)
    scratch += flow(ny, nx, zhn // 2 * tile)
    scratch += [pltpu.VMEM((n, small, 128), F32) for n in (NC, nx, ny, zln, zhn)]
    scratch += [
        pltpu.VMEM((small, 128), F32),
        pltpu.VMEM((zln, zrows, dz), BF),
        pltpu.VMEM((zln, zrows, dz), BF),
        pltpu.VMEM((zhn, zrows, dz), BF),
        pltpu.VMEM((zhn, tile, dz), BF),
        pltpu.VMEM((zhn, tile, dz), BF),
        pltpu.VMEM((zln, tile, dz), BF),
        pltpu.VMEM((tile, chan), F32),
        pltpu.VMEM((NC, nx, ny, 2 * rs, dz), BF),
        pltpu.VMEM((NC, ny, nx, rp, dz), BF),
        pltpu.SemaphoreType.DMA((5,)),
        pltpu.SemaphoreType.DMA((1,)),
        pltpu.SemaphoreType.DMA((96,)),
        pltpu.SemaphoreType.DMA((96,)),
    ]
    any_spec = pl.BlockSpec(memory_space=pl.ANY)
    vmem = pl.BlockSpec(memory_space=pltpu.VMEM)
    out = pl.pallas_call(
        functools.partial(kernel, g),
        out_shape=(
            jax.ShapeDtypeStruct((rows_in, chan), BF),
            jax.ShapeDtypeStruct((rpd, chan), F32),
            jax.ShapeDtypeStruct((1, chan), F32),
            jax.ShapeDtypeStruct((chan, dz), F32),
            jax.ShapeDtypeStruct((2, book // zln, dz), BF),
            jax.ShapeDtypeStruct((2, book // zln), F32),
        ),
        in_specs=[any_spec, vmem, any_spec, vmem, any_spec, any_spec],
        out_specs=(any_spec, vmem, vmem, vmem, vmem, vmem),
        scratch_shapes=scratch,
        compiler_params=pltpu.CompilerParams(
            collective_id=0, has_side_effects=True, vmem_limit_bytes=56 << 20),
    )(feats, codes, conv_weight, conv_bias.reshape(1, chan), proj_weight, codebooks)
    fg, cg, bg, pg, cm, cu = out
    return fg, cg, bg.reshape(chan), pg, cm, cu


def solution(mesh, g=None):
    if g is None:
        g = {"nx": 4, "ny": 4, "zh": 4, "zl": 4}
    placed = (P(("dp", "tm"), None), P("dp", None, "tm"), P(), P(), P(), P())
    return jax.shard_map(
        functools.partial(shards, g),
        mesh=mesh,
        in_specs=placed,
        out_specs=(
            P(("dp", "tm"), None),
            P(("dp", "tm"), None),
            P(),
            P(),
            P(None, "tm", None),
            P(None, "tm"),
        ),
        check_vma=False,
    )
```

```python
import functools

import jax
import jax.numpy as jnp
from jax import lax
from jax.experimental import pallas as pl
from jax.experimental.pallas import tpu as pltpu
from jax.sharding import PartitionSpec as P

MESH = pl.DeviceIdType.MESH
BF = jnp.bfloat16
F32 = jnp.float32
NC = 2


def dot(a, b, ca=1, cb=0):
    return lax.dot_general(a, b, (((ca,), (cb,)), ((), ())), preferred_element_type=F32)


class Sems:
    def __init__(self, send, recv):
        self.send, self.recv, self.count, self.started, self.index = send, recv, 0, [], {}

    def copy(self, src, dst, device):
        index = self.count
        self.count += 1
        made = pltpu.make_async_remote_copy(
            src_ref=src, dst_ref=dst, send_sem=self.send.at[index], recv_sem=self.recv.at[index],
            device_id=device, device_id_type=MESH,
        )
        self.index[id(made)] = index
        return made

    def arrived(self, made, ref, device):
        index = self.index[id(made)]
        pltpu.make_async_remote_copy(
            src_ref=ref, dst_ref=ref, send_sem=self.send.at[index], recv_sem=self.recv.at[index],
            device_id=device, device_id_type=MESH,
        ).wait_recv()

    def start(self, src, dst, device):
        made = self.copy(src, dst, device)
        made.start()
        self.started.append(made)
        return made


def kernel(g, feats, codes_in, conv_w, conv_b_in, proj_w, books,
           fg_out, conv_f, sm_f, ag_s, ag_p,
           feats_v, codes, cw_v, conv_b, pw_v, books_v, oh_v, fx, unf, acc_v, hid, lat, lg_v, hgf, halo_v, next_v, fg_f,
           s0_0, s0_c, s0_1, s0_r1, s0_2, s0_r2,
           s1_0, s1_c, s1_1, s1_r1, s1_2, s1_r2,
           pr_0, pr_c, pr_1, pr_r1, pr_2, pr_r2,
           ca_0, ca_c, ca_1, ca_r1, ca_2, ca_r2,
           cb_0, cb_c, cb_1, cb_r1, cb_2, cb_r2,
           sm_c, sm_x, sm_y, sm_l, sm_h,
           zl_s, zl_r, zh_r, ch_s, ch_r, cl_r,
           in_sem, send_sem, recv_sem):
    nx, ny, zh_n, zl_n = g["nx"], g["ny"], g["zh"], g["zl"]
    frames, chan, dz, book = g["frames"], g["chan"], g["dz"], g["book"]
    total = g["total"]
    rs, rp, rpd = g["rs"], g["rp"], g["rpd"]
    tile = zl_n * rpd
    zhh = zh_n // 2
    lanes = chan // 128

    dp, zl = lax.axis_index("dp"), lax.axis_index("tm")
    c = dp % NC
    x = dp // NC % nx
    y = dp // (NC * nx) % ny
    zh = dp // (NC * nx * ny)

    def dev(c_, x_, y_, zh_, zl_):
        return (((zh_ * ny + y_) * nx + x_) * NC + c_, zl_)

    def at_core():
        return dev(1 - c, x, y, zh, zl)

    def at_x(d):
        return dev(c, (x + d) % nx, y, zh, zl)

    def at_y(d):
        return dev(c, x, (y + d) % ny, zh, zl)

    def at_l(d):
        return dev(c, x, y, zh, (zl + d) % zl_n)

    def at_h(d):
        return dev(c, x, y, (zh + d) % zh_n, zl)

    sems = Sems(send_sem, recv_sem)

    barrier = pltpu.get_barrier_semaphore()
    partners = [at_core()]
    for ring, n in ((at_x, nx), (at_y, ny), (at_l, zl_n), (at_h, zh_n)):
        partners += [ring(d) for d in range(1, n)]
    for partner in partners:
        pl.semaphore_signal(barrier, inc=1, device_id=partner, device_id_type=MESH)

    half = 2 * chan
    loads = [
        pltpu.make_async_copy(feats, feats_v, in_sem.at[0]),
        pltpu.make_async_copy(conv_w.at[pl.ds(half, half)], cw_v.at[pl.ds(half, half)], in_sem.at[1]),
        pltpu.make_async_copy(conv_w.at[pl.ds(0, half)], cw_v.at[pl.ds(0, half)], in_sem.at[2]),
        pltpu.make_async_copy(proj_w, pw_v, in_sem.at[3]),
        pltpu.make_async_copy(books, books_v, in_sem.at[4]),
        pltpu.make_async_copy(codes_in, codes, in_sem.at[5]),
        pltpu.make_async_copy(conv_b_in, conv_b, in_sem.at[6]),
    ]
    for load in loads:
        load.start()

    rows_in = 2 * frames
    loads[0].wait()
    for k in range(lanes):
        fx[k, pl.ds(8, rows_in), :] = feats_v[:, k * 128:(k + 1) * 128].astype(F32)

    def spread(start, tap):
        for k in range(lanes):
            piece = fx[k, pl.ds(start, frames, stride=2), :]
            unf[:, tap * chan + k * 128:tap * chan + (k + 1) * 128] = piece.astype(BF)

    spread(8, 2)
    spread(9, 3)
    loads[1].wait()
    acc_v[...] = dot(unf[:, half:], cw_v[half:, :])

    pl.semaphore_wait(barrier, len(partners))
    halo = sems.copy(feats_v.at[pl.ds(rows_in - 16, 16)], halo_v, at_l(1))

    @pl.when(zl < zl_n - 1)
    def _():
        halo.start()

    small_rows = book // 128

    def onehot(level):
        eye = (lax.broadcasted_iota(jnp.int32, (frames, frames), 0)
               == lax.broadcasted_iota(jnp.int32, (frames, frames), 1))
        column = jnp.sum(jnp.where(eye, code_rows[level:level + 1, :], 0.0), 1, keepdims=True)
        lane = lax.broadcasted_iota(jnp.int32, (frames, 128), 1).astype(F32)
        for r in range(small_rows):
            block = (column - r * 128.0 == lane).astype(F32)
            oh_v[:, r * 128:(r + 1) * 128] = block.astype(BF)
            sm_c[0, pl.ds(level * small_rows + r, 1), :] = jnp.sum(block, 0, keepdims=True)

    per_q = book // zl_n
    per_c = nx * ny * rs

    def onehot_t(level, side):
        rows = nx * ny * zl_n * rs
        p = lax.broadcasted_iota(jnp.int32, (rows, 1), 0)
        i = p % rs
        q = p // rs % zl_n
        if level == 0:
            yy = p // (rs * zl_n) % ny
            xx = p // (rs * zl_n * ny)
        else:
            xx = p // (rs * zl_n) % nx
            yy = p // (rs * zl_n * nx)
        ids = q * per_q + side * per_c + (xx * ny + yy) * rs + i
        return (ids.astype(F32) == code_rows[level:level + 1, :]).astype(F32).astype(BF)

    @pl.when(zl == 0)
    def _():
        halo_v[...] = jnp.zeros(halo_v.shape, BF)

    @pl.when(zl > 0)
    def _():
        halo.wait_recv()

    last = halo_v[...].astype(F32)[8:16, :]
    for k in range(lanes):
        fx[k, pl.ds(0, 8), :] = last[:, k * 128:(k + 1) * 128]
    spread(6, 0)
    spread(7, 1)
    loads[2].wait()
    loads[6].wait()
    conv = acc_v[...] + dot(unf[:, :half], cw_v[:half, :])
    hid[...] = (conv + conv_b[...]).astype(BF)
    loads[3].wait()
    lat[...] = dot(hid[...], pw_v[...])

    loads[5].wait()
    code_rows = codes[0].astype(F32)

    def level_sums(level, ref0, refc):
        value = lat[...].astype(BF)

        def part(side):
            made = dot(onehot_t(level, side), value)
            ref0[side] = made.astype(BF).reshape(ref0.shape[1:])

        part(1 - c)
        copy = sems.start(ref0.at[1 - c], refc, at_core())
        part(c)
        return copy

    s0_core = level_sums(0, s0_0, s0_c)
    onehot(0)
    loads[4].wait()
    lat[...] = lat[...] - dot(oh_v[...], books_v[0])
    s1_core = level_sums(1, s1_0, s1_c)

    def stage1(core_copy, ref0, refc, ref1, refr, ring, n, me):
        core_copy.wait_recv()
        ref1[...] = (ref0[c].astype(F32) + refc[...].astype(F32)).astype(BF)
        return [sems.start(ref1.at[(me + d) % n], refr.at[d - 1], ring(d)) for d in range(1, n)]

    def stage2(copies, ref1, refr, ref2, refr2, ring, n, me, me1):
        made = ref1[me1].astype(F32)
        for d, copy in enumerate(copies):
            copy.wait_recv()
            made = made + refr[d].astype(F32)
        ref2[...] = made.astype(BF).reshape(ref2.shape)
        return [sems.start(ref2.at[(me + d) % n], refr2.at[d - 1], ring(d)) for d in range(1, n)]

    def finish(copies, ref2, refr2, me):
        made = ref2[me].astype(F32)
        for d, copy in enumerate(copies):
            copy.wait_recv()
            made = made + refr2[d].astype(F32)
        return made

    onehot(1)
    value = lat[...]
    lg = (value + (value - dot(oh_v[...], books_v[1]))).astype(BF)
    lg_v[...] = lg
    pr_0[...] = dot(hid[...], lg, 0, 0).astype(BF).reshape(pr_0.shape)
    pr_core = sems.start(pr_0.at[1 - c], pr_c, at_core())

    s0_x = stage1(s0_core, s0_0, s0_c, s0_1, s0_r1, at_x, nx, x)
    s1_y = stage1(s1_core, s1_0, s1_c, s1_1, s1_r1, at_y, ny, y)

    hg = dot(lg, pw_v[...], 1, 1).astype(BF)
    hid[...] = hg
    hgw = hg.astype(F32)
    hgf[pl.ds(0, frames), :] = hgw
    nxt = sems.copy(hid.at[pl.ds(0, 16)], next_v, at_l(-1 + zl_n))

    @pl.when(zl > 0)
    def _():
        nxt.start()

    bias = jnp.sum(hgw, 0, keepdims=True)
    for r in range(lanes):
        sm_c[0, pl.ds(2 * small_rows + r, 1), :] = bias[:, r * 128:(r + 1) * 128]
    pad = sm_c.shape[1] - 2 * small_rows - lanes
    if pad:
        sm_c[0, pl.ds(2 * small_rows + lanes, pad), :] = jnp.zeros((pad, 128), F32)
    sm_core = sems.start(sm_c.at[0], sm_c.at[1], at_core())

    def corr(base, ref0, x_first):
        group = ny * nx * NC * tile
        for zz in range(zhh):
            start = base + zz * group
            made = dot(unf[:, start:start + group], lg_v[...], 0, 0).astype(BF)
            for yy in range(ny):
                for xx in range(nx):
                    for cc in range(NC):
                        at = ((yy * nx + xx) * NC + cc) * tile
                        a, b = (xx, yy) if x_first else (yy, xx)
                        row = (b * zhh + zz) * tile
                        ref0[cc, a, row:row + tile, :] = made[at:at + tile, :]

    pr_x = stage1(pr_core, pr_0, pr_c, pr_1, pr_r1, at_x, nx, x)
    corr(0, ca_0, True)
    ca_core = sems.start(ca_0.at[1 - c], ca_c, at_core())
    corr(half, cb_0, False)
    cb_core = sems.start(cb_0.at[1 - c], cb_c, at_core())

    def small(copies, ref, me, n, nxt_ref):
        for copy in copies:
            copy.wait_recv()
        made = None
        for j in range(n):
            piece = ref[(me - j + n) % n]
            made = piece if made is None else made + piece
        nxt_ref[...] = made

    def small_send(ref, ring, n):
        return [sems.start(ref.at[0], ref.at[d], ring(d)) for d in range(1, n)]

    small([sm_core], sm_c, c, NC, sm_x.at[0])
    sm_xs = small_send(sm_x, at_x, nx)

    s0_y = stage2(s0_x, s0_1, s0_r1, s0_2, s0_r2, at_y, ny, y, x)
    s1_x = stage2(s1_y, s1_1, s1_r1, s1_2, s1_r2, at_x, nx, x, y)
    pr_y = stage2(pr_x, pr_1, pr_r1, pr_2, pr_r2, at_y, ny, y, x)
    small(sm_xs, sm_x, x, nx, sm_y.at[0])
    sm_ys = small_send(sm_y, at_y, ny)
    ca_x = stage1(ca_core, ca_0, ca_c, ca_1, ca_r1, at_x, nx, x)
    cb_y = stage1(cb_core, cb_0, cb_c, cb_1, cb_r1, at_y, ny, y)

    s0_d = finish(s0_y, s0_2, s0_r2, y)
    s1_d = finish(s1_x, s1_2, s1_r2, x)
    pr_d = finish(pr_y, pr_2, pr_r2, y)
    for q in range(zl_n):
        zl_s[q] = jnp.concatenate(
            [s0_d[q * rs:(q + 1) * rs], s1_d[q * rs:(q + 1) * rs], pr_d], 0).astype(BF)
    zl_c = [sems.start(zl_s.at[(zl + d) % zl_n], zl_r.at[d], at_l(d)) for d in range(1, zl_n)]
    zl_r[0] = zl_s[zl]
    small(sm_ys, sm_y, y, ny, sm_l.at[0])
    sm_ls = small_send(sm_l, at_l, zl_n)

    @pl.when(zl == zl_n - 1)
    def _():
        next_v[...] = jnp.zeros(next_v.shape, BF)

    @pl.when(zl < zl_n - 1)
    def _():
        nxt.wait_recv()

    hgf[pl.ds(frames, 8), :] = next_v[...].astype(F32)[0:8, :]
    lg_next = hgf[pl.ds(1, frames), :].astype(BF)

    def feat_part(part):
        made = (dot(lg_next, cw_v[pl.ds(part * chan, chan), :], 1, 1)
                + dot(hid[...], cw_v[pl.ds(half + part * chan, chan), :], 1, 1))
        for k in range(lanes):
            fg_f[k, pl.ds(part, frames, stride=2), :] = made[:, k * 128:(k + 1) * 128]

    feat_part(0)
    feat_part(1)

    def summed(copies, ref, me, n):
        for copy in copies:
            copy.wait_recv()
        made = None
        for j in range(n):
            piece = ref[(me - j + n) % n].astype(F32)
            made = piece if made is None else made + piece
        return made

    zh_r[0] = summed(zl_c, zl_r, zl, zl_n).astype(BF)
    zh_c = [sems.start(zh_r.at[0], zh_r.at[d], at_h(d)) for d in range(1, zh_n)]
    small(sm_ls, sm_l, zl, zl_n, sm_h.at[0])
    sm_hs = small_send(sm_h, at_h, zh_n)

    ca_y = stage2(ca_x, ca_1, ca_r1, ca_2, ca_r2, at_y, ny, y, x)
    cb_x = stage2(cb_y, cb_1, cb_r1, cb_2, cb_r2, at_x, nx, x, y)

    for k in range(lanes):
        fg_out[:, k * 128:(k + 1) * 128] = fg_f[k].astype(BF)

    ca_d = finish(ca_y, ca_2, ca_r2, y)
    cb_d = finish(cb_x, cb_2, cb_r2, x)
    for zz in range(zhh):
        ch_s[zz] = ca_d[zz * tile:(zz + 1) * tile].astype(BF)
        ch_s[zhh + zz] = cb_d[zz * tile:(zz + 1) * tile].astype(BF)
    ch_c = [sems.start(ch_s.at[(zh + d) % zh_n], ch_r.at[d], at_h(d)) for d in range(1, zh_n)]
    ch_r[0] = ch_s[zh]

    small(sm_hs, sm_h, zh, zh_n, sm_f)
    q_rows = per_q // 128
    base = c * per_c + (x * ny + y) * rs
    ids = lax.broadcasted_iota(jnp.int32, (rs, 128), 1) - lax.broadcasted_iota(jnp.int32, (rs, 128), 0)
    columns = []
    for level in range(2):
        row = sm_f[pl.ds(level * small_rows + zl * q_rows + base // 128, 1), :]
        columns.append(jnp.sum(jnp.where(ids == base % 128, row, 0.0), 1, keepdims=True))
    counts = jnp.maximum(jnp.concatenate(columns, 0), 1.0)

    done = summed(zh_c, zh_r, zh, zh_n)
    ag_s[c, x, y] = (done[:2 * rs] / counts).astype(BF)
    ag_p[c, y, x] = done[2 * rs:].astype(BF)
    gs = [sems.start(ag_s.at[c, x, y], ag_s.at[c, x, y], at_y(d)) for d in range(1, ny)]
    gp = [sems.start(ag_p.at[c, y, x], ag_p.at[c, y, x], at_x(d)) for d in range(1, nx)]

    def gathered(sem_copies, ref_of, n, me):
        for d, copy in enumerate(sem_copies):
            src = (me - (d + 1) + n) % n
            sems.arrived(copy, ref_of(src), at_core())

    gathered(gs, lambda j: ag_s.at[c, x, j], ny, y)
    gs2 = [sems.start(ag_s.at[c, x], ag_s.at[c, x], at_x(d)) for d in range(1, nx)]
    gathered(gp, lambda j: ag_p.at[c, y, j], nx, x)
    gp2 = [sems.start(ag_p.at[c, y], ag_p.at[c, y], at_y(d)) for d in range(1, ny)]
    gs3 = [(x, sems.start(ag_s.at[c, x], ag_s.at[c, x], at_core()))]
    gp3 = [(y, sems.start(ag_p.at[c, y], ag_p.at[c, y], at_core()))]

    cl_r[0] = summed(ch_c, ch_r, zh, zh_n).astype(BF)
    cl_c = [sems.start(cl_r.at[0], cl_r.at[d], at_l(d)) for d in range(1, zl_n)]

    for d in range(1, max(nx, ny)):
        if d < nx:
            j = (x - d + nx) % nx
            sems.arrived(gs2[d - 1], ag_s.at[c, j], at_core())
            gs3.append((j, sems.start(ag_s.at[c, j], ag_s.at[c, j], at_core())))
        if d < ny:
            j = (y - d + ny) % ny
            sems.arrived(gp2[d - 1], ag_p.at[c, j], at_core())
            gp3.append((j, sems.start(ag_p.at[c, j], ag_p.at[c, j], at_core())))

    owned = summed(cl_c, cl_r, zl, zl_n)
    top = owned.astype(BF)
    low = (owned - top.astype(F32)).astype(BF)
    conv_f[...] = (dot(top, pw_v[...], 1, 1) + dot(low, pw_v[...], 1, 1)) / total
    for j, copy in gs3:
        sems.arrived(copy, ag_s.at[1 - c, j], at_core())
    for j, copy in gp3:
        sems.arrived(copy, ag_p.at[1 - c, j], at_core())

    for copy in sems.started:
        copy.wait_send()

    @pl.when(zl < zl_n - 1)
    def _():
        halo.wait_send()

    @pl.when(zl > 0)
    def _():
        nxt.wait_send()


def assemble(g, fg_in, conv_f, sm_f, ag_s, ag_p, fg_out, conv_out, bias_out, proj_out, means_out, usage_out):
    nx, ny, zl_n, book, total = g["nx"], g["ny"], g["zl"], g["book"], g["total"]
    rs, rp, rpd, lanes = g["rs"], g["rp"], g["rpd"], g["chan"] // 128
    zl = lax.axis_index("tm")
    fg_out[...] = fg_in[...]
    picked = None
    for q in range(zl_n):
        piece = jnp.where(zl == q, conv_f[q * rpd:(q + 1) * rpd, :], 0.0)
        picked = piece if picked is None else picked + piece
    conv_out[...] = picked
    small_rows = book // 128
    q_rows = small_rows // zl_n
    per_c = nx * ny * rs
    for level in range(2):
        for r in range(q_rows):
            count = sm_f[pl.ds(level * small_rows + zl * q_rows + r, 1), :]
            usage_out[level:level + 1, r * 128:(r + 1) * 128] = count * (book / total)
    for r in range(lanes):
        bias_out[:, r * 128:(r + 1) * 128] = sm_f[2 * small_rows + r:2 * small_rows + r + 1, :] / total
    for cc in range(NC):
        for xx in range(nx):
            for level in range(2):
                rows = [ag_s[cc, xx, yy].astype(F32)[level * rs:(level + 1) * rs] for yy in range(ny)]
                at = cc * per_c + xx * ny * rs
                means_out[level, at:at + ny * rs, :] = jnp.concatenate(rows, 0).astype(BF)
            for yy in range(ny):
                at = ((cc * nx + xx) * ny + yy) * rp
                proj_out[at:at + rp, :] = ag_p[cc, yy, xx].astype(F32) * (1.0 / total)


def shards(g, feats, codes, conv_weight, conv_bias, proj_weight, codebooks):
    rows_in, chan = feats.shape
    frames = rows_in // 2
    dz = proj_weight.shape[1]
    book = codebooks.shape[1]
    nx, ny, zhn, zln = g["nx"], g["ny"], g["zh"], g["zl"]
    devices = NC * nx * ny * zhn * zln
    taps = conv_weight.shape[0]
    g = dict(g, frames=frames, chan=chan, dz=dz, book=book, total=float(frames * devices),
             rs=book // (NC * nx * ny * zln), rp=chan // (NC * nx * ny), rpd=taps // devices)
    rs, rp, rpd = g["rs"], g["rp"], g["rpd"]
    tile = zln * rpd
    lanes = chan // 128

    def flow(a, b, rows):
        return [
            pltpu.VMEM((NC, a, b * rows, dz), BF),
            pltpu.VMEM((a, b * rows, dz), BF),
            pltpu.VMEM((a, b * rows, dz), BF),
            pltpu.VMEM((max(a - 1, 1), b * rows, dz), BF),
            pltpu.VMEM((b, rows, dz), BF),
            pltpu.VMEM((max(b - 1, 1), rows, dz), BF),
        ]

    small = -(-(2 * book // 128 + lanes) // 8) * 8
    zrows = 2 * rs + rp
    scratch = [
        pltpu.VMEM((rows_in, chan), BF),
        pltpu.VMEM((1, 2, frames), jnp.int32),
        pltpu.VMEM((taps, chan), BF),
        pltpu.VMEM((1, chan), F32),
        pltpu.VMEM((chan, dz), BF),
        pltpu.VMEM((2, book, dz), BF),
        pltpu.VMEM((frames, book), BF),
        pltpu.VMEM((lanes, rows_in + 8, 128), F32),
        pltpu.VMEM((frames, taps), BF),
        pltpu.VMEM((frames, chan), F32),
        pltpu.VMEM((frames, chan), BF),
        pltpu.VMEM((frames, dz), F32),
        pltpu.VMEM((frames, dz), BF),
        pltpu.VMEM((frames + 8, chan), F32),
        pltpu.VMEM((16, chan), BF),
        pltpu.VMEM((16, chan), BF),
        pltpu.VMEM((lanes, rows_in, 128), F32),
    ]
    scratch += flow(nx, ny, zln * rs)
    scratch += flow(ny, nx, zln * rs)
    scratch += flow(nx, ny, rp)
    scratch += flow(nx, ny, zhn // 2 * tile)
    scratch += flow(ny, nx, zhn // 2 * tile)
    scratch += [pltpu.VMEM((n, small, 128), F32) for n in (NC, nx, ny, zln, zhn)]
    scratch += [
        pltpu.VMEM((zln, zrows, dz), BF),
        pltpu.VMEM((zln, zrows, dz), BF),
        pltpu.VMEM((zhn, zrows, dz), BF),
        pltpu.VMEM((zhn, tile, dz), BF),
        pltpu.VMEM((zhn, tile, dz), BF),
        pltpu.VMEM((zln, tile, dz), BF),
        pltpu.SemaphoreType.DMA((7,)),
        pltpu.SemaphoreType.DMA((96,)),
        pltpu.SemaphoreType.DMA((96,)),
    ]
    hbm = pl.BlockSpec(memory_space=pltpu.HBM)
    vmem = pl.BlockSpec(memory_space=pltpu.VMEM)
    fg, conv_f, sm_f, ag_s, ag_p = pl.pallas_call(
        functools.partial(kernel, g),
        out_shape=(
            pltpu.VMEM((rows_in, chan), BF),
            pltpu.VMEM((tile, chan), F32),
            pltpu.VMEM((small, 128), F32),
            pltpu.VMEM((NC, nx, ny, 2 * rs, dz), BF),
            pltpu.VMEM((NC, ny, nx, rp, dz), BF),
        ),
        in_specs=[hbm] * 6,
        out_specs=(vmem,) * 5,
        scratch_shapes=scratch,
        compiler_params=pltpu.CompilerParams(
            collective_id=0, has_side_effects=True, vmem_limit_bytes=32 << 20),
    )(*[pltpu.with_memory_space_constraint(v, pltpu.HBM) for v in (
        feats, codes, conv_weight, conv_bias.reshape(1, chan), proj_weight, codebooks)])
    fg, cg, bg, pg, cm, cu = pl.pallas_call(
        functools.partial(assemble, g),
        out_shape=(
            jax.ShapeDtypeStruct((rows_in, chan), BF),
            jax.ShapeDtypeStruct((rpd, chan), F32),
            jax.ShapeDtypeStruct((1, chan), F32),
            jax.ShapeDtypeStruct((chan, dz), F32),
            jax.ShapeDtypeStruct((2, book // zln, dz), BF),
            jax.ShapeDtypeStruct((2, book // zln), F32),
        ),
        in_specs=[vmem, vmem, vmem, vmem, vmem],
        out_specs=(vmem, vmem, vmem, vmem, vmem, vmem),
        compiler_params=pltpu.CompilerParams(vmem_limit_bytes=8 << 20),
    )(fg, conv_f, sm_f, ag_s, ag_p)
    return fg, cg, bg.reshape(chan), pg, cm, cu


def solution(mesh, g=None):
    if g is None:
        g = {"nx": 4, "ny": 4, "zh": 4, "zl": 4}
    placed = (P(("dp", "tm"), None), P("dp", None, "tm"), P(), P(), P(), P())
    return jax.shard_map(
        functools.partial(shards, g),
        mesh=mesh,
        in_specs=placed,
        out_specs=(
            P(("dp", "tm"), None),
            P(("dp", "tm"), None),
            P(),
            P(),
            P(None, "tm", None),
            P(None, "tm"),
        ),
        check_vma=False,
    )
```

```python
import functools

import jax
import jax.numpy as jnp
from jax import lax
from jax.experimental import pallas as pl
from jax.experimental.pallas import tpu as pltpu
from jax.sharding import PartitionSpec as P

MESH = pl.DeviceIdType.MESH
BF = jnp.bfloat16
F32 = jnp.float32
NC = 2


def dot(a, b, ca=1, cb=0):
    return lax.dot_general(a, b, (((ca,), (cb,)), ((), ())), preferred_element_type=F32)


class Sems:
    def __init__(self, send, recv):
        self.send, self.recv, self.count, self.started, self.index = send, recv, 0, [], {}

    def copy(self, src, dst, device):
        index = self.count
        self.count += 1
        made = pltpu.make_async_remote_copy(
            src_ref=src, dst_ref=dst, send_sem=self.send.at[index], recv_sem=self.recv.at[index],
            device_id=device, device_id_type=MESH,
        )
        self.index[id(made)] = index
        return made

    def arrived(self, made, ref, device):
        index = self.index[id(made)]
        pltpu.make_async_remote_copy(
            src_ref=ref, dst_ref=ref, send_sem=self.send.at[index], recv_sem=self.recv.at[index],
            device_id=device, device_id_type=MESH,
        ).wait_recv()

    def start(self, src, dst, device):
        made = self.copy(src, dst, device)
        made.start()
        self.started.append(made)
        return made


def kernel(g, feats, codes_in, conv_w, conv_b_in, proj_w, books,
           fg_out, conv_f, sm_f, ag_s, ag_p,
           feats_v, codes, cw_v, conv_b, pw_v, books_v, oh_v, oht_v, fx, unf, acc_v, hid, lat, lg_v, hgf, halo_v, next_v, fg_f,
           s0_0, s0_c, s0_1, s0_r1, s0_2, s0_r2,
           s1_0, s1_c, s1_1, s1_r1, s1_2, s1_r2,
           pr_0, pr_c, pr_1, pr_r1, pr_2, pr_r2,
           ca_0, ca_c, ca_1, ca_r1, ca_2, ca_r2,
           cb_0, cb_c, cb_1, cb_r1, cb_2, cb_r2,
           sm_c, sm_x, sm_y, sm_t, sm_q, sm_l, sm_h,
           zl_s, zl_r, zh_r, ch_s, ch_r, cl_r,
           in_sem, word_sem, send_sem, recv_sem):
    nx, ny, zh_n, zl_n = g["nx"], g["ny"], g["zh"], g["zl"]
    frames, chan, dz, book = g["frames"], g["chan"], g["dz"], g["book"]
    total = g["total"]
    rs, rp, rpd = g["rs"], g["rp"], g["rpd"]
    tile = zl_n * rpd
    zhh = zh_n // 2
    lanes = chan // 128

    dp, zl = lax.axis_index("dp"), lax.axis_index("tm")
    c = dp % NC
    x = dp // NC % nx
    y = dp // (NC * nx) % ny
    zh = dp // (NC * nx * ny)

    def dev(c_, x_, y_, zh_, zl_):
        return (((zh_ * ny + y_) * nx + x_) * NC + c_, zl_)

    def at_core():
        return dev(1 - c, x, y, zh, zl)

    def at_x(d):
        return dev(c, (x + d) % nx, y, zh, zl)

    def at_y(d):
        return dev(c, x, (y + d) % ny, zh, zl)

    def at_l(d):
        return dev(c, x, y, zh, (zl + d) % zl_n)

    def at_h(d):
        return dev(c, x, y, (zh + d) % zh_n, zl)

    sems = Sems(send_sem, recv_sem)

    half = 2 * chan
    loads = [
        pltpu.make_async_copy(feats, feats_v, in_sem.at[0]),
        pltpu.make_async_copy(conv_w.at[pl.ds(half, half)], cw_v.at[pl.ds(half, half)], in_sem.at[1]),
        pltpu.make_async_copy(conv_w.at[pl.ds(0, half)], cw_v.at[pl.ds(0, half)], in_sem.at[2]),
        pltpu.make_async_copy(proj_w, pw_v, in_sem.at[3]),
        pltpu.make_async_copy(books, books_v, in_sem.at[4]),
        pltpu.make_async_copy(codes_in, codes, in_sem.at[5]),
        pltpu.make_async_copy(conv_b_in, conv_b, in_sem.at[6]),
    ]
    for load in loads:
        load.start()

    ring_z = zh_n * zl_n
    z = zh * zl_n + zl

    def at_z(d):
        zz = (z + d + ring_z) % ring_z
        return dev(c, x, y, zz // zl_n, zz % zl_n)

    reaches = [1]
    while 2 * reaches[-1] < ring_z // 2:
        reaches.append(2 * reaches[-1])
    barrier = pltpu.get_barrier_semaphore()
    partners = [at_core(), at_z(1), at_z(-1)]
    for ring, n in ((at_x, nx), (at_y, ny), (at_l, zl_n)):
        partners += [ring(d) for d in range(1, n)]
    for partner in partners:
        pl.semaphore_signal(barrier, inc=1, device_id=partner, device_id_type=MESH)

    rows_in = 2 * frames
    loads[0].wait()
    for k in range(lanes):
        fx[k, pl.ds(8, rows_in), :] = feats_v[:, k * 128:(k + 1) * 128].astype(F32)

    def spread(start, tap):
        for k in range(lanes):
            piece = fx[k, pl.ds(start, frames, stride=2), :]
            unf[:, tap * chan + k * 128:tap * chan + (k + 1) * 128] = piece.astype(BF)

    spread(8, 2)
    spread(9, 3)
    loads[5].wait()
    loads[1].wait()
    code_rows = codes[0].astype(F32)

    small_rows = book // 128

    def onehot(level):
        eye = (lax.broadcasted_iota(jnp.int32, (frames, frames), 0)
               == lax.broadcasted_iota(jnp.int32, (frames, frames), 1))
        column = jnp.sum(jnp.where(eye, code_rows[level:level + 1, :], 0.0), 1, keepdims=True)
        lane = lax.broadcasted_iota(jnp.int32, (frames, 128), 1).astype(F32)
        for r in range(small_rows):
            block = (column - r * 128.0 == lane).astype(F32)
            oh_v[level, :, r * 128:(r + 1) * 128] = block.astype(BF)
            sm_c[0, pl.ds(level * small_rows + r, 1), :] = jnp.sum(block, 0, keepdims=True)

    per_q = book // zl_n
    per_c = nx * ny * rs

    def onehot_t(level, side):
        rows = nx * ny * zl_n * rs
        p = lax.broadcasted_iota(jnp.int32, (rows, 1), 0)
        i = p % rs
        q = p // rs % zl_n
        if level == 0:
            yy = p // (rs * zl_n) % ny
            xx = p // (rs * zl_n * ny)
        else:
            xx = p // (rs * zl_n) % nx
            yy = p // (rs * zl_n * nx)
        ids = q * per_q + side * per_c + (xx * ny + yy) * rs + i
        return (ids.astype(F32) == code_rows[level:level + 1, :]).astype(F32).astype(BF)

    acc_v[...] = dot(unf[:, half:], cw_v[half:, :])
    for level in range(2):
        onehot(level)
        for side in range(NC):
            oht_v[level, side] = onehot_t(level, side)

    pl.semaphore_wait(barrier, len(partners))

    def tell(k):
        if k < len(reaches):
            for d in (reaches[k], -reaches[k]):
                pl.semaphore_signal(word_sem.at[k], inc=1, device_id=at_z(d), device_id_type=MESH)

    def told(k):
        if k < len(reaches):
            pl.semaphore_wait(word_sem.at[k], 2)

    tell(0)
    halo = sems.copy(feats_v.at[pl.ds(rows_in - 16, 16)], halo_v, at_l(1))

    @pl.when(zl < zl_n - 1)
    def _():
        halo.start()

    @pl.when(zl == 0)
    def _():
        halo_v[...] = jnp.zeros(halo_v.shape, BF)

    @pl.when(zl > 0)
    def _():
        halo.wait_recv()

    last = halo_v[...].astype(F32)[8:16, :]
    for k in range(lanes):
        fx[k, pl.ds(0, 8), :] = last[:, k * 128:(k + 1) * 128]
    spread(6, 0)
    spread(7, 1)
    loads[2].wait()
    loads[6].wait()
    conv = acc_v[...] + dot(unf[:, :half], cw_v[:half, :])
    hid[...] = (conv + conv_b[...]).astype(BF)
    told(0)
    tell(1)
    loads[3].wait()
    lat[...] = dot(hid[...], pw_v[...])

    def level_sums(level, ref0, refc):
        value = lat[...].astype(BF)

        def part(side):
            made = dot(oht_v[level, side], value)
            ref0[side] = made.astype(BF).reshape(ref0.shape[1:])

        part(1 - c)
        copy = sems.start(ref0.at[1 - c], refc, at_core())
        part(c)
        return copy

    def stage1(core_copy, ref0, refc, ref1, refr, ring, n, me):
        core_copy.wait_recv()
        ref1[...] = (ref0[c].astype(F32) + refc[...].astype(F32)).astype(BF)
        return [sems.start(ref1.at[(me + d) % n], refr.at[d - 1], ring(d)) for d in range(1, n)]

    def stage2(copies, ref1, refr, ref2, refr2, ring, n, me, me1):
        made = ref1[me1].astype(F32)
        for d, copy in enumerate(copies):
            copy.wait_recv()
            made = made + refr[d].astype(F32)
        ref2[...] = made.astype(BF).reshape(ref2.shape)
        return [sems.start(ref2.at[(me + d) % n], refr2.at[d - 1], ring(d)) for d in range(1, n)]

    def finish(copies, ref2, refr2, me):
        made = ref2[me].astype(F32)
        for d, copy in enumerate(copies):
            copy.wait_recv()
            made = made + refr2[d].astype(F32)
        return made

    s0_core = level_sums(0, s0_0, s0_c)
    loads[4].wait()
    lat[...] = lat[...] - dot(oh_v[0], books_v[0])
    s1_core = level_sums(1, s1_0, s1_c)

    s0_x = stage1(s0_core, s0_0, s0_c, s0_1, s0_r1, at_x, nx, x)

    value = lat[...]
    lg = (value + (value - dot(oh_v[1], books_v[1]))).astype(BF)
    lg_v[...] = lg
    pr_0[...] = dot(hid[...], lg, 0, 0).astype(BF).reshape(pr_0.shape)
    pr_core = sems.start(pr_0.at[1 - c], pr_c, at_core())
    told(1)
    tell(2)
    s1_y = stage1(s1_core, s1_0, s1_c, s1_1, s1_r1, at_y, ny, y)

    hg = dot(lg, pw_v[...], 1, 1).astype(BF)
    hid[...] = hg
    hgw = hg.astype(F32)
    hgf[pl.ds(0, frames), :] = hgw
    nxt = sems.copy(hid.at[pl.ds(0, 16)], next_v, at_l(-1 + zl_n))

    @pl.when(zl > 0)
    def _():
        nxt.start()

    bias = jnp.sum(hgw, 0, keepdims=True)
    for r in range(lanes):
        sm_c[0, pl.ds(2 * small_rows + r, 1), :] = bias[:, r * 128:(r + 1) * 128]
    pad = sm_c.shape[1] - 2 * small_rows - lanes
    if pad:
        sm_c[0, pl.ds(2 * small_rows + lanes, pad), :] = jnp.zeros((pad, 128), F32)
    sm_core = sems.start(sm_c.at[0], sm_c.at[1], at_core())

    def corr(base, ref0, x_first):
        group = ny * nx * NC * tile
        for zz in range(zhh):
            start = base + zz * group
            made = dot(unf[:, start:start + group], lg_v[...], 0, 0).astype(BF)
            for yy in range(ny):
                for xx in range(nx):
                    for cc in range(NC):
                        at = ((yy * nx + xx) * NC + cc) * tile
                        a, b = (xx, yy) if x_first else (yy, xx)
                        row = (b * zhh + zz) * tile
                        ref0[cc, a, row:row + tile, :] = made[at:at + tile, :]

    corr(0, ca_0, True)
    ca_core = sems.start(ca_0.at[1 - c], ca_c, at_core())
    pr_x = stage1(pr_core, pr_0, pr_c, pr_1, pr_r1, at_x, nx, x)
    corr(half, cb_0, False)
    cb_core = sems.start(cb_0.at[1 - c], cb_c, at_core())

    def small(copies, ref, me, n, nxt_ref):
        for copy in copies:
            copy.wait_recv()
        made = None
        for j in range(n):
            piece = ref[(me - j + n) % n]
            made = piece if made is None else made + piece
        nxt_ref[...] = made

    def small_send(ref, ring, n):
        return [sems.start(ref.at[0], ref.at[d], ring(d)) for d in range(1, n)]

    small([sm_core], sm_c, c, NC, sm_x.at[0])
    sm_xs = small_send(sm_x, at_x, nx)

    s0_y = stage2(s0_x, s0_1, s0_r1, s0_2, s0_r2, at_y, ny, y, x)
    s1_x = stage2(s1_y, s1_1, s1_r1, s1_2, s1_r2, at_x, nx, x, y)
    pr_y = stage2(pr_x, pr_1, pr_r1, pr_2, pr_r2, at_y, ny, y, x)
    small(sm_xs, sm_x, x, nx, sm_y.at[0])
    sm_ys = small_send(sm_y, at_y, ny)
    ca_x = stage1(ca_core, ca_0, ca_c, ca_1, ca_r1, at_x, nx, x)
    cb_y = stage1(cb_core, cb_0, cb_c, cb_1, cb_r1, at_y, ny, y)

    @pl.when(zl == zl_n - 1)
    def _():
        next_v[...] = jnp.zeros(next_v.shape, BF)

    @pl.when(zl < zl_n - 1)
    def _():
        nxt.wait_recv()

    hgf[pl.ds(frames, 8), :] = next_v[...].astype(F32)[0:8, :]
    lg_next = hgf[pl.ds(1, frames), :].astype(BF)

    def feat_part(part):
        made = (dot(lg_next, cw_v[pl.ds(part * chan, chan), :], 1, 1)
                + dot(hid[...], cw_v[pl.ds(half + part * chan, chan), :], 1, 1))
        for k in range(lanes):
            fg_f[k, pl.ds(part, frames, stride=2), :] = made[:, k * 128:(k + 1) * 128]

    feat_part(0)

    s0_d = finish(s0_y, s0_2, s0_r2, y)
    s1_d = finish(s1_x, s1_2, s1_r2, x)
    pr_d = finish(pr_y, pr_2, pr_r2, y)
    for q in range(zl_n):
        zl_s[q] = jnp.concatenate(
            [s0_d[q * rs:(q + 1) * rs], s1_d[q * rs:(q + 1) * rs], pr_d], 0).astype(BF)
    zl_c = [sems.start(zl_s.at[(zl + d) % zl_n], zl_r.at[d], at_l(d)) for d in range(1, zl_n)]
    zl_r[0] = zl_s[zl]
    small(sm_ys, sm_y, y, ny, sm_t)
    q_rows = per_q // 128
    for q in range(zl_n):
        for level in range(2):
            at = level * small_rows + q * q_rows
            sm_q[q, level * q_rows:(level + 1) * q_rows, :] = sm_t[at:at + q_rows, :]
        sm_q[q, 2 * q_rows:2 * q_rows + lanes, :] = sm_t[2 * small_rows:2 * small_rows + lanes, :]
        rest = sm_q.shape[1] - 2 * q_rows - lanes
        if rest:
            sm_q[q, 2 * q_rows + lanes:, :] = jnp.zeros((rest, 128), F32)
    sm_ls = [sems.start(sm_q.at[(zl + d) % zl_n], sm_l.at[d], at_l(d)) for d in range(1, zl_n)]
    sm_l[0] = sm_q[zl]

    def summed(copies, ref, me, n):
        for copy in copies:
            copy.wait_recv()
        made = None
        for j in range(n):
            piece = ref[(me - j + n) % n].astype(F32)
            made = piece if made is None else made + piece
        return made

    ca_y = stage2(ca_x, ca_1, ca_r1, ca_2, ca_r2, at_y, ny, y, x)
    cb_x = stage2(cb_y, cb_1, cb_r1, cb_2, cb_r2, at_x, nx, x, y)

    told(2)
    zh_r[0] = summed(zl_c, zl_r, zl, zl_n).astype(BF)
    zh_c = [sems.start(zh_r.at[0], zh_r.at[d], at_h(d)) for d in range(1, zh_n)]
    small(sm_ls, sm_l, zl, zl_n, sm_h.at[0])
    sm_hs = small_send(sm_h, at_h, zh_n)

    ca_d = finish(ca_y, ca_2, ca_r2, y)
    cb_d = finish(cb_x, cb_2, cb_r2, x)
    for zz in range(zhh):
        ch_s[zz] = ca_d[zz * tile:(zz + 1) * tile].astype(BF)
        ch_s[zhh + zz] = cb_d[zz * tile:(zz + 1) * tile].astype(BF)
    ch_c = [sems.start(ch_s.at[(zh + d) % zh_n], ch_r.at[d], at_h(d)) for d in range(1, zh_n)]
    ch_r[0] = ch_s[zh]

    feat_part(1)
    for k in range(lanes):
        fg_out[:, k * 128:(k + 1) * 128] = fg_f[k].astype(BF)

    small(sm_hs, sm_h, zh, zh_n, sm_f)
    base = c * per_c + (x * ny + y) * rs
    ids = lax.broadcasted_iota(jnp.int32, (rs, 128), 1) - lax.broadcasted_iota(jnp.int32, (rs, 128), 0)
    columns = []
    for level in range(2):
        row = sm_f[pl.ds(level * q_rows + base // 128, 1), :]
        columns.append(jnp.sum(jnp.where(ids == base % 128, row, 0.0), 1, keepdims=True))
    counts = jnp.maximum(jnp.concatenate(columns, 0), 1.0)

    done = summed(zh_c, zh_r, zh, zh_n)
    ag_s[c, x, y] = (done[:2 * rs] / counts).astype(BF)
    ag_p[c, y, x] = done[2 * rs:].astype(BF)
    gs = [sems.start(ag_s.at[c, x, y], ag_s.at[c, x, y], at_y(d)) for d in range(1, ny)]
    gp = [sems.start(ag_p.at[c, y, x], ag_p.at[c, y, x], at_x(d)) for d in range(1, nx)]

    def gathered(sem_copies, ref_of, n, me):
        for d, copy in enumerate(sem_copies):
            src = (me - (d + 1) + n) % n
            sems.arrived(copy, ref_of(src), at_core())

    gathered(gs, lambda j: ag_s.at[c, x, j], ny, y)
    gs2 = [sems.start(ag_s.at[c, x], ag_s.at[c, x], at_x(d)) for d in range(1, nx)]
    gathered(gp, lambda j: ag_p.at[c, y, j], nx, x)
    gp2 = [sems.start(ag_p.at[c, y], ag_p.at[c, y], at_y(d)) for d in range(1, ny)]
    gs3 = [(x, sems.start(ag_s.at[c, x], ag_s.at[c, x], at_core()))]
    gp3 = [(y, sems.start(ag_p.at[c, y], ag_p.at[c, y], at_core()))]

    cl_r[0] = summed(ch_c, ch_r, zh, zh_n).astype(BF)
    cl_c = [sems.start(cl_r.at[0], cl_r.at[d], at_l(d)) for d in range(1, zl_n)]

    for d in range(1, max(nx, ny)):
        if d < nx:
            j = (x - d + nx) % nx
            sems.arrived(gs2[d - 1], ag_s.at[c, j], at_core())
            gs3.append((j, sems.start(ag_s.at[c, j], ag_s.at[c, j], at_core())))
        if d < ny:
            j = (y - d + ny) % ny
            sems.arrived(gp2[d - 1], ag_p.at[c, j], at_core())
            gp3.append((j, sems.start(ag_p.at[c, j], ag_p.at[c, j], at_core())))

    owned = summed(cl_c, cl_r, zl, zl_n)
    top = owned.astype(BF)
    low = (owned - top.astype(F32)).astype(BF)
    conv_f[...] = (dot(top, pw_v[...], 1, 1) + dot(low, pw_v[...], 1, 1)) / total
    for j, copy in gs3:
        sems.arrived(copy, ag_s.at[1 - c, j], at_core())
    for j, copy in gp3:
        sems.arrived(copy, ag_p.at[1 - c, j], at_core())

    for copy in sems.started:
        copy.wait_send()

    @pl.when(zl < zl_n - 1)
    def _():
        halo.wait_send()

    @pl.when(zl > 0)
    def _():
        nxt.wait_send()


def assemble(g, fg_in, conv_f, sm_f, ag_s, ag_p, fg_out, conv_out, bias_out, proj_out, means_out, usage_out):
    nx, ny, zl_n, book, total = g["nx"], g["ny"], g["zl"], g["book"], g["total"]
    rs, rp, rpd, lanes = g["rs"], g["rp"], g["rpd"], g["chan"] // 128
    zl = lax.axis_index("tm")
    fg_out[...] = fg_in[...]
    picked = None
    for q in range(zl_n):
        piece = jnp.where(zl == q, conv_f[q * rpd:(q + 1) * rpd, :], 0.0)
        picked = piece if picked is None else picked + piece
    conv_out[...] = picked
    small_rows = book // 128
    q_rows = small_rows // zl_n
    per_c = nx * ny * rs
    for level in range(2):
        for r in range(q_rows):
            count = sm_f[level * q_rows + r:level * q_rows + r + 1, :]
            usage_out[level:level + 1, r * 128:(r + 1) * 128] = count * (book / total)
    for r in range(lanes):
        bias_out[:, r * 128:(r + 1) * 128] = sm_f[2 * q_rows + r:2 * q_rows + r + 1, :] / total
    for cc in range(NC):
        for xx in range(nx):
            for level in range(2):
                rows = [ag_s[cc, xx, yy].astype(F32)[level * rs:(level + 1) * rs] for yy in range(ny)]
                at = cc * per_c + xx * ny * rs
                means_out[level, at:at + ny * rs, :] = jnp.concatenate(rows, 0).astype(BF)
            for yy in range(ny):
                at = ((cc * nx + xx) * ny + yy) * rp
                proj_out[at:at + rp, :] = ag_p[cc, yy, xx].astype(F32) * (1.0 / total)


def shards(g, feats, codes, conv_weight, conv_bias, proj_weight, codebooks):
    rows_in, chan = feats.shape
    frames = rows_in // 2
    dz = proj_weight.shape[1]
    book = codebooks.shape[1]
    nx, ny, zhn, zln = g["nx"], g["ny"], g["zh"], g["zl"]
    devices = NC * nx * ny * zhn * zln
    taps = conv_weight.shape[0]
    g = dict(g, frames=frames, chan=chan, dz=dz, book=book, total=float(frames * devices),
             rs=book // (NC * nx * ny * zln), rp=chan // (NC * nx * ny), rpd=taps // devices)
    rs, rp, rpd = g["rs"], g["rp"], g["rpd"]
    tile = zln * rpd
    lanes = chan // 128

    def flow(a, b, rows):
        return [
            pltpu.VMEM((NC, a, b * rows, dz), BF),
            pltpu.VMEM((a, b * rows, dz), BF),
            pltpu.VMEM((a, b * rows, dz), BF),
            pltpu.VMEM((max(a - 1, 1), b * rows, dz), BF),
            pltpu.VMEM((b, rows, dz), BF),
            pltpu.VMEM((max(b - 1, 1), rows, dz), BF),
        ]

    small = -(-(2 * book // 128 + lanes) // 8) * 8
    few = -(-(2 * book // zln // 128 + lanes) // 8) * 8
    zrows = 2 * rs + rp
    scratch = [
        pltpu.VMEM((rows_in, chan), BF),
        pltpu.VMEM((1, 2, frames), jnp.int32),
        pltpu.VMEM((taps, chan), BF),
        pltpu.VMEM((1, chan), F32),
        pltpu.VMEM((chan, dz), BF),
        pltpu.VMEM((2, book, dz), BF),
        pltpu.VMEM((2, frames, book), BF),
        pltpu.VMEM((2, NC, book // NC, frames), BF),
        pltpu.VMEM((lanes, rows_in + 8, 128), F32),
        pltpu.VMEM((frames, taps), BF),
        pltpu.VMEM((frames, chan), F32),
        pltpu.VMEM((frames, chan), BF),
        pltpu.VMEM((frames, dz), F32),
        pltpu.VMEM((frames, dz), BF),
        pltpu.VMEM((frames + 8, chan), F32),
        pltpu.VMEM((16, chan), BF),
        pltpu.VMEM((16, chan), BF),
        pltpu.VMEM((lanes, rows_in, 128), F32),
    ]
    scratch += flow(nx, ny, zln * rs)
    scratch += flow(ny, nx, zln * rs)
    scratch += flow(nx, ny, rp)
    scratch += flow(nx, ny, zhn // 2 * tile)
    scratch += flow(ny, nx, zhn // 2 * tile)
    scratch += [pltpu.VMEM((n, small, 128), F32) for n in (NC, nx, ny)] + [pltpu.VMEM((small, 128), F32)]
    scratch += [pltpu.VMEM((n, few, 128), F32) for n in (zln, zln, zhn)]
    scratch += [
        pltpu.VMEM((zln, zrows, dz), BF),
        pltpu.VMEM((zln, zrows, dz), BF),
        pltpu.VMEM((zhn, zrows, dz), BF),
        pltpu.VMEM((zhn, tile, dz), BF),
        pltpu.VMEM((zhn, tile, dz), BF),
        pltpu.VMEM((zln, tile, dz), BF),
        pltpu.SemaphoreType.DMA((7,)),
        pltpu.SemaphoreType.REGULAR((3,)),
        pltpu.SemaphoreType.DMA((96,)),
        pltpu.SemaphoreType.DMA((96,)),
    ]
    hbm = pl.BlockSpec(memory_space=pltpu.HBM)
    vmem = pl.BlockSpec(memory_space=pltpu.VMEM)
    fg, conv_f, sm_f, ag_s, ag_p = pl.pallas_call(
        functools.partial(kernel, g),
        out_shape=(
            pltpu.VMEM((rows_in, chan), BF),
            pltpu.VMEM((tile, chan), F32),
            pltpu.VMEM((few, 128), F32),
            pltpu.VMEM((NC, nx, ny, 2 * rs, dz), BF),
            pltpu.VMEM((NC, ny, nx, rp, dz), BF),
        ),
        in_specs=[hbm] * 6,
        out_specs=(vmem,) * 5,
        scratch_shapes=scratch,
        compiler_params=pltpu.CompilerParams(
            collective_id=0, has_side_effects=True, vmem_limit_bytes=32 << 20),
    )(*[pltpu.with_memory_space_constraint(v, pltpu.HBM) for v in (
        feats, codes, conv_weight, conv_bias.reshape(1, chan), proj_weight, codebooks)])
    fg, cg, bg, pg, cm, cu = pl.pallas_call(
        functools.partial(assemble, g),
        out_shape=(
            jax.ShapeDtypeStruct((rows_in, chan), BF),
            jax.ShapeDtypeStruct((rpd, chan), F32),
            jax.ShapeDtypeStruct((1, chan), F32),
            jax.ShapeDtypeStruct((chan, dz), F32),
            jax.ShapeDtypeStruct((2, book // zln, dz), BF),
            jax.ShapeDtypeStruct((2, book // zln), F32),
        ),
        in_specs=[vmem, vmem, vmem, vmem, vmem],
        out_specs=(vmem, vmem, vmem, vmem, vmem, vmem),
        compiler_params=pltpu.CompilerParams(vmem_limit_bytes=8 << 20),
    )(fg, conv_f, sm_f, ag_s, ag_p)
    return fg, cg, bg.reshape(chan), pg, cm, cu


def solution(mesh, g=None):
    if g is None:
        g = {"nx": 4, "ny": 4, "zh": 4, "zl": 4}
    placed = (P(("dp", "tm"), None), P("dp", None, "tm"), P(), P(), P(), P())
    return jax.shard_map(
        functools.partial(shards, g),
        mesh=mesh,
        in_specs=placed,
        out_specs=(
            P(("dp", "tm"), None),
            P(("dp", "tm"), None),
            P(),
            P(),
            P(None, "tm", None),
            P(None, "tm"),
        ),
        check_vma=False,
    )
```

```python
import functools

import jax
import jax.numpy as jnp
from jax import lax
from jax.experimental import pallas as pl
from jax.experimental.pallas import tpu as pltpu
from jax.sharding import PartitionSpec as P

MESH = pl.DeviceIdType.MESH
BF = jnp.bfloat16
F32 = jnp.float32
NC = 2


def far_first(n):
    return sorted(range(1, n), key=lambda d: -min(d, n - d))


def dot(a, b, ca=1, cb=0):
    return lax.dot_general(a, b, (((ca,), (cb,)), ((), ())), preferred_element_type=F32)


class Sems:
    def __init__(self, send, recv):
        self.send, self.recv, self.count, self.started, self.index = send, recv, 0, [], {}

    def copy(self, src, dst, device):
        index = self.count
        self.count += 1
        made = pltpu.make_async_remote_copy(
            src_ref=src, dst_ref=dst, send_sem=self.send.at[index], recv_sem=self.recv.at[index],
            device_id=device, device_id_type=MESH,
        )
        self.index[id(made)] = index
        return made

    def ring(self, n, src, dst, device):
        made = {d: self.start(src(d), dst(d), device(d)) for d in far_first(n)}
        return [made[d] for d in range(1, n)]

    def arrived(self, made, ref, device):
        index = self.index[id(made)]
        pltpu.make_async_remote_copy(
            src_ref=ref, dst_ref=ref, send_sem=self.send.at[index], recv_sem=self.recv.at[index],
            device_id=device, device_id_type=MESH,
        ).wait_recv()

    def start(self, src, dst, device):
        made = self.copy(src, dst, device)
        made.start()
        self.started.append(made)
        return made


def kernel(g, feats, codes_in, conv_w, conv_b_in, proj_w, books,
           fg_out, conv_f, sm_f, ag,
           feats_v, codes, cw_v, conv_b, pw_v, books_v, oh_v, oht_v, fx, unf, acc_v, hid, lat, lg_v, hgf, halo_v, next_v, fg_f,
           s0_0, s0_c, s0_1, s0_r1, s0_2, s0_r2,
           s1_0, s1_c, s1_1, s1_r1, s1_2, s1_r2,
           pr_0, pr_c, pr_1, pr_r1, pr_2, pr_r2,
           ca_0, ca_c, ca_1, ca_r1, ca_2, ca_r2,
           cb_0, cb_c, cb_1, cb_r1, cb_2, cb_r2,
           sm_c, sm_x, sm_y, sm_t, sm_q, sm_l, sm_h,
           zl_s, zl_r, zh_r, ch_s, ch_r, cl_r,
           in_sem, word_sem, send_sem, recv_sem):
    nx, ny, zh_n, zl_n = g["nx"], g["ny"], g["zh"], g["zl"]
    frames, chan, dz, book = g["frames"], g["chan"], g["dz"], g["book"]
    total = g["total"]
    rs, rp, rpd = g["rs"], g["rp"], g["rpd"]
    tile = zl_n * rpd
    zhh = zh_n // 2
    lanes = chan // 128

    dp, zl = lax.axis_index("dp"), lax.axis_index("tm")
    c = dp % NC
    x = dp // NC % nx
    y = dp // (NC * nx) % ny
    zh = dp // (NC * nx * ny)

    def dev(c_, x_, y_, zh_, zl_):
        return (((zh_ * ny + y_) * nx + x_) * NC + c_, zl_)

    def at_core():
        return dev(1 - c, x, y, zh, zl)

    def at_x(d):
        return dev(c, (x + d) % nx, y, zh, zl)

    def at_y(d):
        return dev(c, x, (y + d) % ny, zh, zl)

    def at_l(d):
        return dev(c, x, y, zh, (zl + d) % zl_n)

    def at_h(d):
        return dev(c, x, y, (zh + d) % zh_n, zl)

    sems = Sems(send_sem, recv_sem)

    half = 2 * chan
    loads = [
        pltpu.make_async_copy(feats, feats_v, in_sem.at[0]),
        pltpu.make_async_copy(conv_w.at[pl.ds(half, half)], cw_v.at[pl.ds(half, half)], in_sem.at[1]),
        pltpu.make_async_copy(conv_w.at[pl.ds(0, half)], cw_v.at[pl.ds(0, half)], in_sem.at[2]),
        pltpu.make_async_copy(proj_w, pw_v, in_sem.at[3]),
        pltpu.make_async_copy(books, books_v, in_sem.at[4]),
        pltpu.make_async_copy(codes_in, codes, in_sem.at[5]),
        pltpu.make_async_copy(conv_b_in, conv_b, in_sem.at[6]),
    ]
    for load in loads:
        load.start()

    ring_z = zh_n * zl_n
    z = zh * zl_n + zl

    def at_z(d):
        zz = (z + d + ring_z) % ring_z
        return dev(c, x, y, zz // zl_n, zz % zl_n)

    reaches = [1]
    while 2 * reaches[-1] < ring_z // 2:
        reaches.append(2 * reaches[-1])
    barrier = pltpu.get_barrier_semaphore()
    partners = [at_core(), at_z(1), at_z(-1)]
    for ring, n in ((at_x, nx), (at_y, ny), (at_l, zl_n)):
        partners += [ring(d) for d in range(1, n)]
    for partner in partners:
        pl.semaphore_signal(barrier, inc=1, device_id=partner, device_id_type=MESH)

    rows_in = 2 * frames
    loads[0].wait()
    for k in range(lanes):
        fx[k, pl.ds(8, rows_in), :] = feats_v[:, k * 128:(k + 1) * 128].astype(F32)

    def spread(start, tap):
        for k in range(lanes):
            piece = fx[k, pl.ds(start, frames, stride=2), :]
            unf[:, tap * chan + k * 128:tap * chan + (k + 1) * 128] = piece.astype(BF)

    spread(8, 2)
    spread(9, 3)
    loads[5].wait()
    loads[1].wait()
    code_rows = codes[0].astype(F32)

    small_rows = book // 128

    def onehot(level):
        eye = (lax.broadcasted_iota(jnp.int32, (frames, frames), 0)
               == lax.broadcasted_iota(jnp.int32, (frames, frames), 1))
        column = jnp.sum(jnp.where(eye, code_rows[level:level + 1, :], 0.0), 1, keepdims=True)
        lane = lax.broadcasted_iota(jnp.int32, (frames, 128), 1).astype(F32)
        for r in range(small_rows):
            block = (column - r * 128.0 == lane).astype(F32)
            oh_v[level, :, r * 128:(r + 1) * 128] = block.astype(BF)
            sm_c[0, pl.ds(level * small_rows + r, 1), :] = jnp.sum(block, 0, keepdims=True)

    per_q = book // zl_n
    per_c = nx * ny * rs

    def onehot_t(level, side):
        rows = nx * ny * zl_n * rs
        p = lax.broadcasted_iota(jnp.int32, (rows, 1), 0)
        i = p % rs
        q = p // rs % zl_n
        if level == 0:
            yy = p // (rs * zl_n) % ny
            xx = p // (rs * zl_n * ny)
        else:
            xx = p // (rs * zl_n) % nx
            yy = p // (rs * zl_n * nx)
        ids = q * per_q + side * per_c + (xx * ny + yy) * rs + i
        return (ids.astype(F32) == code_rows[level:level + 1, :]).astype(F32).astype(BF)

    acc_v[...] = dot(unf[:, half:], cw_v[half:, :])
    for level in range(2):
        onehot(level)
        for side in range(NC):
            oht_v[level, side] = onehot_t(level, side)

    pl.semaphore_wait(barrier, len(partners))

    def tell(k):
        if k < len(reaches):
            for d in (reaches[k], -reaches[k]):
                pl.semaphore_signal(word_sem.at[k], inc=1, device_id=at_z(d), device_id_type=MESH)

    def told(k):
        if k < len(reaches):
            pl.semaphore_wait(word_sem.at[k], 2)

    tell(0)
    halo = sems.copy(feats_v.at[pl.ds(rows_in - 16, 16)], halo_v, at_l(1))

    @pl.when(zl < zl_n - 1)
    def _():
        halo.start()

    @pl.when(zl == 0)
    def _():
        halo_v[...] = jnp.zeros(halo_v.shape, BF)

    @pl.when(zl > 0)
    def _():
        halo.wait_recv()

    last = halo_v[...].astype(F32)[8:16, :]
    for k in range(lanes):
        fx[k, pl.ds(0, 8), :] = last[:, k * 128:(k + 1) * 128]
    spread(6, 0)
    spread(7, 1)
    loads[2].wait()
    loads[6].wait()
    conv = acc_v[...] + dot(unf[:, :half], cw_v[:half, :])
    hid[...] = (conv + conv_b[...]).astype(BF)
    told(0)
    tell(1)
    loads[3].wait()
    lat[...] = dot(hid[...], pw_v[...])

    def level_sums(level, ref0, refc):
        value = lat[...].astype(BF)

        def part(side):
            made = dot(oht_v[level, side], value)
            ref0[side] = made.astype(BF).reshape(ref0.shape[1:])

        part(1 - c)
        copy = sems.start(ref0.at[1 - c], refc, at_core())
        part(c)
        return copy

    def stage1(core_copy, ref0, refc, ref1, refr, ring, n, me):
        core_copy.wait_recv()
        ref1[...] = (ref0[c].astype(F32) + refc[...].astype(F32)).astype(BF)
        return sems.ring(n, lambda d: ref1.at[(me + d) % n], lambda d: refr.at[d - 1], ring)

    def stage2(copies, ref1, refr, ref2, refr2, ring, n, me, me1):
        made = ref1[me1].astype(F32)
        for d, copy in enumerate(copies):
            copy.wait_recv()
            made = made + refr[d].astype(F32)
        ref2[...] = made.astype(BF).reshape(ref2.shape)
        return sems.ring(n, lambda d: ref2.at[(me + d) % n], lambda d: refr2.at[d - 1], ring)

    def finish(copies, ref2, refr2, me):
        made = ref2[me].astype(F32)
        for d, copy in enumerate(copies):
            copy.wait_recv()
            made = made + refr2[d].astype(F32)
        return made

    s0_core = level_sums(0, s0_0, s0_c)
    loads[4].wait()
    lat[...] = lat[...] - dot(oh_v[0], books_v[0])
    s1_core = level_sums(1, s1_0, s1_c)

    s0_x = stage1(s0_core, s0_0, s0_c, s0_1, s0_r1, at_x, nx, x)

    value = lat[...]
    lg = (value + (value - dot(oh_v[1], books_v[1]))).astype(BF)
    lg_v[...] = lg
    pr_0[...] = dot(hid[...], lg, 0, 0).astype(BF).reshape(pr_0.shape)
    pr_core = sems.start(pr_0.at[1 - c], pr_c, at_core())
    told(1)
    tell(2)
    s1_y = stage1(s1_core, s1_0, s1_c, s1_1, s1_r1, at_y, ny, y)

    hg = dot(lg, pw_v[...], 1, 1).astype(BF)
    hid[...] = hg
    hgw = hg.astype(F32)
    hgf[pl.ds(0, frames), :] = hgw
    nxt = sems.copy(hid.at[pl.ds(0, 16)], next_v, at_l(-1 + zl_n))

    @pl.when(zl > 0)
    def _():
        nxt.start()

    bias = jnp.sum(hgw, 0, keepdims=True)
    for r in range(lanes):
        sm_c[0, pl.ds(2 * small_rows + r, 1), :] = bias[:, r * 128:(r + 1) * 128]
    pad = sm_c.shape[1] - 2 * small_rows - lanes
    if pad:
        sm_c[0, pl.ds(2 * small_rows + lanes, pad), :] = jnp.zeros((pad, 128), F32)
    sm_core = sems.start(sm_c.at[0], sm_c.at[1], at_core())

    def corr(base, ref0, x_first):
        group = ny * nx * NC * tile
        for zz in range(zhh):
            start = base + zz * group
            made = dot(unf[:, start:start + group], lg_v[...], 0, 0).astype(BF)
            for yy in range(ny):
                for xx in range(nx):
                    for cc in range(NC):
                        at = ((yy * nx + xx) * NC + cc) * tile
                        a, b = (xx, yy) if x_first else (yy, xx)
                        row = (b * zhh + zz) * tile
                        ref0[cc, a, row:row + tile, :] = made[at:at + tile, :]

    corr(0, ca_0, True)
    ca_core = sems.start(ca_0.at[1 - c], ca_c, at_core())
    pr_x = stage1(pr_core, pr_0, pr_c, pr_1, pr_r1, at_x, nx, x)
    corr(half, cb_0, False)
    cb_core = sems.start(cb_0.at[1 - c], cb_c, at_core())

    def small(copies, ref, me, n, nxt_ref):
        for copy in copies:
            copy.wait_recv()
        made = None
        for j in range(n):
            piece = ref[(me - j + n) % n]
            made = piece if made is None else made + piece
        nxt_ref[...] = made

    def small_send(ref, ring, n):
        return sems.ring(n, lambda d: ref.at[0], lambda d: ref.at[d], ring)

    small([sm_core], sm_c, c, NC, sm_x.at[0])
    sm_xs = small_send(sm_x, at_x, nx)

    s0_y = stage2(s0_x, s0_1, s0_r1, s0_2, s0_r2, at_y, ny, y, x)
    s1_x = stage2(s1_y, s1_1, s1_r1, s1_2, s1_r2, at_x, nx, x, y)
    pr_y = stage2(pr_x, pr_1, pr_r1, pr_2, pr_r2, at_y, ny, y, x)
    small(sm_xs, sm_x, x, nx, sm_y.at[0])
    sm_ys = small_send(sm_y, at_y, ny)
    ca_x = stage1(ca_core, ca_0, ca_c, ca_1, ca_r1, at_x, nx, x)
    cb_y = stage1(cb_core, cb_0, cb_c, cb_1, cb_r1, at_y, ny, y)

    @pl.when(zl == zl_n - 1)
    def _():
        next_v[...] = jnp.zeros(next_v.shape, BF)

    @pl.when(zl < zl_n - 1)
    def _():
        nxt.wait_recv()

    hgf[pl.ds(frames, 8), :] = next_v[...].astype(F32)[0:8, :]
    lg_next = hgf[pl.ds(1, frames), :].astype(BF)

    def feat_part(part):
        made = (dot(lg_next, cw_v[pl.ds(part * chan, chan), :], 1, 1)
                + dot(hid[...], cw_v[pl.ds(half + part * chan, chan), :], 1, 1))
        for k in range(lanes):
            fg_f[k, pl.ds(part, frames, stride=2), :] = made[:, k * 128:(k + 1) * 128]

    feat_part(0)

    s0_d = finish(s0_y, s0_2, s0_r2, y)
    s1_d = finish(s1_x, s1_2, s1_r2, x)
    pr_d = finish(pr_y, pr_2, pr_r2, y)
    for q in range(zl_n):
        zl_s[q] = jnp.concatenate(
            [s0_d[q * rs:(q + 1) * rs], s1_d[q * rs:(q + 1) * rs], pr_d], 0).astype(BF)
    zl_c = sems.ring(zl_n, lambda d: zl_s.at[(zl + d) % zl_n], lambda d: zl_r.at[d], at_l)
    zl_r[0] = zl_s[zl]
    small(sm_ys, sm_y, y, ny, sm_t)
    q_rows = per_q // 128
    for q in range(zl_n):
        for level in range(2):
            at = level * small_rows + q * q_rows
            sm_q[q, level * q_rows:(level + 1) * q_rows, :] = sm_t[at:at + q_rows, :]
        sm_q[q, 2 * q_rows:2 * q_rows + lanes, :] = sm_t[2 * small_rows:2 * small_rows + lanes, :]
        rest = sm_q.shape[1] - 2 * q_rows - lanes
        if rest:
            sm_q[q, 2 * q_rows + lanes:, :] = jnp.zeros((rest, 128), F32)
    sm_ls = [sems.start(sm_q.at[(zl + d) % zl_n], sm_l.at[d], at_l(d)) for d in range(1, zl_n)]
    sm_l[0] = sm_q[zl]

    def summed(copies, ref, me, n):
        for copy in copies:
            copy.wait_recv()
        made = None
        for j in range(n):
            piece = ref[(me - j + n) % n].astype(F32)
            made = piece if made is None else made + piece
        return made

    ca_y = stage2(ca_x, ca_1, ca_r1, ca_2, ca_r2, at_y, ny, y, x)
    cb_x = stage2(cb_y, cb_1, cb_r1, cb_2, cb_r2, at_x, nx, x, y)

    told(2)
    zh_r[0] = summed(zl_c, zl_r, zl, zl_n).astype(BF)
    zh_c = sems.ring(zh_n, lambda d: zh_r.at[0], lambda d: zh_r.at[d], at_h)
    small(sm_ls, sm_l, zl, zl_n, sm_h.at[0])
    sm_hs = small_send(sm_h, at_h, zh_n)

    ca_d = finish(ca_y, ca_2, ca_r2, y)
    cb_d = finish(cb_x, cb_2, cb_r2, x)
    for zz in range(zhh):
        ch_s[zz] = ca_d[zz * tile:(zz + 1) * tile].astype(BF)
        ch_s[zhh + zz] = cb_d[zz * tile:(zz + 1) * tile].astype(BF)
    ch_c = sems.ring(zh_n, lambda d: ch_s.at[(zh + d) % zh_n], lambda d: ch_r.at[d], at_h)
    ch_r[0] = ch_s[zh]

    feat_part(1)
    for k in range(lanes):
        fg_out[:, k * 128:(k + 1) * 128] = fg_f[k].astype(BF)

    small(sm_hs, sm_h, zh, zh_n, sm_f)
    base = c * per_c + (x * ny + y) * rs
    ids = lax.broadcasted_iota(jnp.int32, (rs, 128), 1) - lax.broadcasted_iota(jnp.int32, (rs, 128), 0)
    columns = []
    for level in range(2):
        row = sm_f[pl.ds(level * q_rows + base // 128, 1), :]
        columns.append(jnp.sum(jnp.where(ids == base % 128, row, 0.0), 1, keepdims=True))
    counts = jnp.maximum(jnp.concatenate(columns, 0), 1.0)

    done = summed(zh_c, zh_r, zh, zh_n)
    ag[c, x, y] = jnp.concatenate([done[:2 * rs] / counts, done[2 * rs:]], 0).astype(BF)
    steps = [(dx, dy) for dx in range(nx) for dy in range(ny) if dx or dy]
    steps.sort(key=lambda s: -(min(s[0], nx - s[0]) + min(s[1], ny - s[1])))
    plane = {
        (dx, dy): sems.start(ag.at[c, x, y], ag.at[c, x, y], dev(c, (x + dx) % nx, (y + dy) % ny, zh, zl))
        for dx, dy in steps
    }

    cl_r[0] = summed(ch_c, ch_r, zh, zh_n).astype(BF)
    cl_c = [sems.start(cl_r.at[0], cl_r.at[d], at_l(d)) for d in range(1, zl_n)]

    rows_in_order = sorted(range(nx), key=lambda d: min(d, nx - d))
    others = []
    for dx in rows_in_order:
        j = (x - dx + nx) % nx
        for dy in range(ny):
            if dx or dy:
                sems.arrived(plane[dx, dy], ag.at[c, j, (y - dy + ny) % ny], at_core())
        others.append((j, sems.start(ag.at[c, j], ag.at[c, j], at_core())))

    owned = summed(cl_c, cl_r, zl, zl_n)
    top = owned.astype(BF)
    low = (owned - top.astype(F32)).astype(BF)
    conv_f[...] = (dot(top, pw_v[...], 1, 1) + dot(low, pw_v[...], 1, 1)) / total
    for j, copy in others:
        sems.arrived(copy, ag.at[1 - c, j], at_core())

    for copy in sems.started:
        copy.wait_send()

    @pl.when(zl < zl_n - 1)
    def _():
        halo.wait_send()

    @pl.when(zl > 0)
    def _():
        nxt.wait_send()


def assemble(g, fg_in, conv_f, sm_f, ag, fg_out, conv_out, bias_out, proj_out, means_out, usage_out):
    nx, ny, zl_n, book, total = g["nx"], g["ny"], g["zl"], g["book"], g["total"]
    rs, rp, rpd, lanes = g["rs"], g["rp"], g["rpd"], g["chan"] // 128
    zl = lax.axis_index("tm")
    fg_out[...] = fg_in[...]
    picked = None
    for q in range(zl_n):
        piece = jnp.where(zl == q, conv_f[q * rpd:(q + 1) * rpd, :], 0.0)
        picked = piece if picked is None else picked + piece
    conv_out[...] = picked
    small_rows = book // 128
    q_rows = small_rows // zl_n
    per_c = nx * ny * rs
    for level in range(2):
        for r in range(q_rows):
            count = sm_f[level * q_rows + r:level * q_rows + r + 1, :]
            usage_out[level:level + 1, r * 128:(r + 1) * 128] = count * (book / total)
    for r in range(lanes):
        bias_out[:, r * 128:(r + 1) * 128] = sm_f[2 * q_rows + r:2 * q_rows + r + 1, :] / total
    for cc in range(NC):
        for xx in range(nx):
            for level in range(2):
                rows = [ag[cc, xx, yy].astype(F32)[level * rs:(level + 1) * rs] for yy in range(ny)]
                at = cc * per_c + xx * ny * rs
                means_out[level, at:at + ny * rs, :] = jnp.concatenate(rows, 0).astype(BF)
            for yy in range(ny):
                at = ((cc * nx + xx) * ny + yy) * rp
                proj_out[at:at + rp, :] = ag[cc, xx, yy].astype(F32)[2 * rs:] * (1.0 / total)


def shards(g, feats, codes, conv_weight, conv_bias, proj_weight, codebooks):
    rows_in, chan = feats.shape
    frames = rows_in // 2
    dz = proj_weight.shape[1]
    book = codebooks.shape[1]
    nx, ny, zhn, zln = g["nx"], g["ny"], g["zh"], g["zl"]
    devices = NC * nx * ny * zhn * zln
    taps = conv_weight.shape[0]
    g = dict(g, frames=frames, chan=chan, dz=dz, book=book, total=float(frames * devices),
             rs=book // (NC * nx * ny * zln), rp=chan // (NC * nx * ny), rpd=taps // devices)
    rs, rp, rpd = g["rs"], g["rp"], g["rpd"]
    tile = zln * rpd
    lanes = chan // 128

    def flow(a, b, rows):
        return [
            pltpu.VMEM((NC, a, b * rows, dz), BF),
            pltpu.VMEM((a, b * rows, dz), BF),
            pltpu.VMEM((a, b * rows, dz), BF),
            pltpu.VMEM((max(a - 1, 1), b * rows, dz), BF),
            pltpu.VMEM((b, rows, dz), BF),
            pltpu.VMEM((max(b - 1, 1), rows, dz), BF),
        ]

    small = -(-(2 * book // 128 + lanes) // 8) * 8
    few = -(-(2 * book // zln // 128 + lanes) // 8) * 8
    zrows = 2 * rs + rp
    scratch = [
        pltpu.VMEM((rows_in, chan), BF),
        pltpu.VMEM((1, 2, frames), jnp.int32),
        pltpu.VMEM((taps, chan), BF),
        pltpu.VMEM((1, chan), F32),
        pltpu.VMEM((chan, dz), BF),
        pltpu.VMEM((2, book, dz), BF),
        pltpu.VMEM((2, frames, book), BF),
        pltpu.VMEM((2, NC, book // NC, frames), BF),
        pltpu.VMEM((lanes, rows_in + 8, 128), F32),
        pltpu.VMEM((frames, taps), BF),
        pltpu.VMEM((frames, chan), F32),
        pltpu.VMEM((frames, chan), BF),
        pltpu.VMEM((frames, dz), F32),
        pltpu.VMEM((frames, dz), BF),
        pltpu.VMEM((frames + 8, chan), F32),
        pltpu.VMEM((16, chan), BF),
        pltpu.VMEM((16, chan), BF),
        pltpu.VMEM((lanes, rows_in, 128), F32),
    ]
    scratch += flow(nx, ny, zln * rs)
    scratch += flow(ny, nx, zln * rs)
    scratch += flow(nx, ny, rp)
    scratch += flow(nx, ny, zhn // 2 * tile)
    scratch += flow(ny, nx, zhn // 2 * tile)
    scratch += [pltpu.VMEM((n, small, 128), F32) for n in (NC, nx, ny)] + [pltpu.VMEM((small, 128), F32)]
    scratch += [pltpu.VMEM((n, few, 128), F32) for n in (zln, zln, zhn)]
    scratch += [
        pltpu.VMEM((zln, zrows, dz), BF),
        pltpu.VMEM((zln, zrows, dz), BF),
        pltpu.VMEM((zhn, zrows, dz), BF),
        pltpu.VMEM((zhn, tile, dz), BF),
        pltpu.VMEM((zhn, tile, dz), BF),
        pltpu.VMEM((zln, tile, dz), BF),
        pltpu.SemaphoreType.DMA((7,)),
        pltpu.SemaphoreType.REGULAR((3,)),
        pltpu.SemaphoreType.DMA((96,)),
        pltpu.SemaphoreType.DMA((96,)),
    ]
    hbm = pl.BlockSpec(memory_space=pltpu.HBM)
    vmem = pl.BlockSpec(memory_space=pltpu.VMEM)
    fg, conv_f, sm_f, ag = pl.pallas_call(
        functools.partial(kernel, g),
        out_shape=(
            pltpu.VMEM((rows_in, chan), BF),
            pltpu.VMEM((tile, chan), F32),
            pltpu.VMEM((few, 128), F32),
            pltpu.VMEM((NC, nx, ny, zrows, dz), BF),
        ),
        in_specs=[hbm] * 6,
        out_specs=(vmem,) * 4,
        scratch_shapes=scratch,
        compiler_params=pltpu.CompilerParams(
            collective_id=0, has_side_effects=True, vmem_limit_bytes=32 << 20),
    )(*[pltpu.with_memory_space_constraint(v, pltpu.HBM) for v in (
        feats, codes, conv_weight, conv_bias.reshape(1, chan), proj_weight, codebooks)])
    fg, cg, bg, pg, cm, cu = pl.pallas_call(
        functools.partial(assemble, g),
        out_shape=(
            jax.ShapeDtypeStruct((rows_in, chan), BF),
            jax.ShapeDtypeStruct((rpd, chan), F32),
            jax.ShapeDtypeStruct((1, chan), F32),
            jax.ShapeDtypeStruct((chan, dz), F32),
            jax.ShapeDtypeStruct((2, book // zln, dz), BF),
            jax.ShapeDtypeStruct((2, book // zln), F32),
        ),
        in_specs=[vmem] * 4,
        out_specs=(vmem, vmem, vmem, vmem, vmem, vmem),
        compiler_params=pltpu.CompilerParams(vmem_limit_bytes=8 << 20),
    )(fg, conv_f, sm_f, ag)
    return fg, cg, bg.reshape(chan), pg, cm, cu


def solution(mesh, g=None):
    if g is None:
        g = {"nx": 4, "ny": 4, "zh": 4, "zl": 4}
    placed = (P(("dp", "tm"), None), P("dp", None, "tm"), P(), P(), P(), P())
    return jax.shard_map(
        functools.partial(shards, g),
        mesh=mesh,
        in_specs=placed,
        out_specs=(
            P(("dp", "tm"), None),
            P(("dp", "tm"), None),
            P(),
            P(),
            P(None, "tm", None),
            P(None, "tm"),
        ),
        check_vma=False,
    )
```

```python
import functools

import jax
import jax.numpy as jnp
from jax import lax
from jax.experimental import pallas as pl
from jax.experimental.pallas import tpu as pltpu
from jax.sharding import PartitionSpec as P

MESH = pl.DeviceIdType.MESH
BF = jnp.bfloat16
F32 = jnp.float32
NC = 2


def far_first(n):
    return sorted(range(1, n), key=lambda d: -min(d, n - d))


def dot(a, b, ca=1, cb=0):
    return lax.dot_general(a, b, (((ca,), (cb,)), ((), ())), preferred_element_type=F32)


class Sems:
    def __init__(self, send, recv):
        self.send, self.recv, self.count, self.started, self.index = send, recv, 0, [], {}

    def copy(self, src, dst, device):
        index = self.count
        self.count += 1
        made = pltpu.make_async_remote_copy(
            src_ref=src, dst_ref=dst, send_sem=self.send.at[index], recv_sem=self.recv.at[index],
            device_id=device, device_id_type=MESH,
        )
        self.index[id(made)] = index
        return made

    def ring(self, n, src, dst, device):
        made = {d: self.start(src(d), dst(d), device(d)) for d in far_first(n)}
        return [made[d] for d in range(1, n)]

    def arrived(self, made, ref, device):
        index = self.index[id(made)]
        pltpu.make_async_remote_copy(
            src_ref=ref, dst_ref=ref, send_sem=self.send.at[index], recv_sem=self.recv.at[index],
            device_id=device, device_id_type=MESH,
        ).wait_recv()

    def start(self, src, dst, device):
        made = self.copy(src, dst, device)
        made.start()
        self.started.append(made)
        return made


def kernel(g, feats, codes_in, conv_w, conv_b_in, proj_w, books,
           fg_out, conv_f, sm_f, ag,
           feats_v, codes, cw_v, conv_b, pw_v, books_v, oh_v, oht_v, fx, unf, acc_v, hid, lat, lg_v, hgf, halo_v, next_v, fg_f,
           s0_0, s0_c, s0_1, s0_r1, s0_2, s0_r2,
           s1_0, s1_c, s1_1, s1_r1, s1_2, s1_r2,
           pr_0, pr_c, pr_1, pr_r1, pr_2, pr_r2,
           ca_0, ca_c, ca_1, ca_r1, ca_2, ca_r2,
           cb_0, cb_c, cb_1, cb_r1, cb_2, cb_r2,
           sm_c, sm_x, sm_y, sm_t, sm_q, sm_l, sm_h,
           zl_s, zl_r, zh_r, ch_s, ch_r, cl_r,
           in_sem, word_sem, send_sem, recv_sem):
    nx, ny, zh_n, zl_n = g["nx"], g["ny"], g["zh"], g["zl"]
    frames, chan, dz, book = g["frames"], g["chan"], g["dz"], g["book"]
    total = g["total"]
    rs, rp, rpd = g["rs"], g["rp"], g["rpd"]
    tile = zl_n * rpd
    zhh = zh_n // 2
    lanes = chan // 128

    dp, zl = lax.axis_index("dp"), lax.axis_index("tm")
    c = dp % NC
    x = dp // NC % nx
    y = dp // (NC * nx) % ny
    zh = dp // (NC * nx * ny)

    def dev(c_, x_, y_, zh_, zl_):
        return (((zh_ * ny + y_) * nx + x_) * NC + c_, zl_)

    def at_core():
        return dev(1 - c, x, y, zh, zl)

    def at_x(d):
        return dev(c, (x + d) % nx, y, zh, zl)

    def at_y(d):
        return dev(c, x, (y + d) % ny, zh, zl)

    def at_l(d):
        return dev(c, x, y, zh, (zl + d) % zl_n)

    def at_h(d):
        return dev(c, x, y, (zh + d) % zh_n, zl)

    sems = Sems(send_sem, recv_sem)

    half = 2 * chan
    loads = [
        pltpu.make_async_copy(feats, feats_v, in_sem.at[0]),
        pltpu.make_async_copy(conv_w.at[pl.ds(half, half)], cw_v.at[pl.ds(half, half)], in_sem.at[1]),
        pltpu.make_async_copy(conv_w.at[pl.ds(0, half)], cw_v.at[pl.ds(0, half)], in_sem.at[2]),
        pltpu.make_async_copy(proj_w, pw_v, in_sem.at[3]),
        pltpu.make_async_copy(books, books_v, in_sem.at[4]),
        pltpu.make_async_copy(codes_in, codes, in_sem.at[5]),
        pltpu.make_async_copy(conv_b_in, conv_b, in_sem.at[6]),
    ]
    for load in loads:
        load.start()

    ring_z = zh_n * zl_n
    z = zh * zl_n + zl

    def at_z(d):
        zz = (z + d + ring_z) % ring_z
        return dev(c, x, y, zz // zl_n, zz % zl_n)

    reaches = [1]
    while 2 * reaches[-1] < ring_z // 2:
        reaches.append(2 * reaches[-1])
    barrier = pltpu.get_barrier_semaphore()
    partners = [at_core(), at_z(1), at_z(-1)]
    for ring, n in ((at_x, nx), (at_y, ny), (at_l, zl_n)):
        partners += [ring(d) for d in range(1, n)]
    for partner in partners:
        pl.semaphore_signal(barrier, inc=1, device_id=partner, device_id_type=MESH)

    rows_in = 2 * frames
    loads[0].wait()
    for k in range(lanes):
        fx[k, pl.ds(8, rows_in), :] = feats_v[:, k * 128:(k + 1) * 128].astype(F32)

    def spread(start, tap):
        for k in range(lanes):
            piece = fx[k, pl.ds(start, frames, stride=2), :]
            unf[:, tap * chan + k * 128:tap * chan + (k + 1) * 128] = piece.astype(BF)

    spread(8, 2)
    spread(9, 3)
    loads[5].wait()
    loads[1].wait()
    code_rows = codes[0].astype(F32)

    small_rows = book // 128

    def onehot(level):
        eye = (lax.broadcasted_iota(jnp.int32, (frames, frames), 0)
               == lax.broadcasted_iota(jnp.int32, (frames, frames), 1))
        column = jnp.sum(jnp.where(eye, code_rows[level:level + 1, :], 0.0), 1, keepdims=True)
        lane = lax.broadcasted_iota(jnp.int32, (frames, 128), 1).astype(F32)
        for r in range(small_rows):
            block = (column - r * 128.0 == lane).astype(F32)
            oh_v[level, :, r * 128:(r + 1) * 128] = block.astype(BF)
            sm_c[0, pl.ds(level * small_rows + r, 1), :] = jnp.sum(block, 0, keepdims=True)

    per_q = book // zl_n
    per_c = nx * ny * rs

    def onehot_t(level, side):
        rows = nx * ny * zl_n * rs
        p = lax.broadcasted_iota(jnp.int32, (rows, 1), 0)
        i = p % rs
        q = p // rs % zl_n
        if level == 0:
            yy = p // (rs * zl_n) % ny
            xx = p // (rs * zl_n * ny)
        else:
            xx = p // (rs * zl_n) % nx
            yy = p // (rs * zl_n * nx)
        ids = q * per_q + side * per_c + (xx * ny + yy) * rs + i
        return (ids.astype(F32) == code_rows[level:level + 1, :]).astype(F32).astype(BF)

    acc_v[...] = dot(unf[:, half:], cw_v[half:, :])
    for level in range(2):
        onehot(level)
        for side in range(NC):
            oht_v[level, side] = onehot_t(level, side)

    pl.semaphore_wait(barrier, len(partners))

    def tell(k):
        if k < len(reaches):
            for d in (reaches[k], -reaches[k]):
                pl.semaphore_signal(word_sem.at[k], inc=1, device_id=at_z(d), device_id_type=MESH)

    def told(k):
        if k < len(reaches):
            pl.semaphore_wait(word_sem.at[k], 2)

    tell(0)
    halo = sems.copy(feats_v.at[pl.ds(rows_in - 16, 16)], halo_v, at_l(1))

    @pl.when(zl < zl_n - 1)
    def _():
        halo.start()

    @pl.when(zl == 0)
    def _():
        halo_v[...] = jnp.zeros(halo_v.shape, BF)

    @pl.when(zl > 0)
    def _():
        halo.wait_recv()

    last = halo_v[...].astype(F32)[8:16, :]
    for k in range(lanes):
        fx[k, pl.ds(0, 8), :] = last[:, k * 128:(k + 1) * 128]
    spread(6, 0)
    spread(7, 1)
    loads[2].wait()
    loads[6].wait()
    conv = acc_v[...] + dot(unf[:, :half], cw_v[:half, :])
    hid[...] = (conv + conv_b[...]).astype(BF)
    told(0)
    tell(1)
    loads[3].wait()
    lat[...] = dot(hid[...], pw_v[...])

    def level_sums(level, ref0, refc):
        value = lat[...].astype(BF)

        def part(side):
            made = dot(oht_v[level, side], value)
            ref0[side] = made.astype(BF).reshape(ref0.shape[1:])

        part(1 - c)
        copy = sems.start(ref0.at[1 - c], refc, at_core())
        part(c)
        return copy

    def stage1(core_copy, ref0, refc, ref1, refr, ring, n, me):
        core_copy.wait_recv()
        ref1[...] = (ref0[c].astype(F32) + refc[...].astype(F32)).astype(BF)
        return sems.ring(n, lambda d: ref1.at[(me + d) % n], lambda d: refr.at[d - 1], ring)

    def stage2(copies, ref1, refr, ref2, refr2, ring, n, me, me1):
        made = ref1[me1].astype(F32)
        for d, copy in enumerate(copies):
            copy.wait_recv()
            made = made + refr[d].astype(F32)
        ref2[...] = made.astype(BF).reshape(ref2.shape)
        return sems.ring(n, lambda d: ref2.at[(me + d) % n], lambda d: refr2.at[d - 1], ring)

    def finish(copies, ref2, refr2, me):
        made = ref2[me].astype(F32)
        for d, copy in enumerate(copies):
            copy.wait_recv()
            made = made + refr2[d].astype(F32)
        return made

    s0_core = level_sums(0, s0_0, s0_c)
    loads[4].wait()
    lat[...] = lat[...] - dot(oh_v[0], books_v[0])
    s1_core = level_sums(1, s1_0, s1_c)

    s0_x = stage1(s0_core, s0_0, s0_c, s0_1, s0_r1, at_x, nx, x)

    value = lat[...]
    lg = (value + (value - dot(oh_v[1], books_v[1]))).astype(BF)
    lg_v[...] = lg
    pr_0[...] = dot(hid[...], lg, 0, 0).astype(BF).reshape(pr_0.shape)
    pr_core = sems.start(pr_0.at[1 - c], pr_c, at_core())
    told(1)
    tell(2)
    s1_y = stage1(s1_core, s1_0, s1_c, s1_1, s1_r1, at_y, ny, y)

    hg = dot(lg, pw_v[...], 1, 1).astype(BF)
    hid[...] = hg
    hgw = hg.astype(F32)
    hgf[pl.ds(0, frames), :] = hgw
    nxt = sems.copy(hid.at[pl.ds(0, 16)], next_v, at_l(-1 + zl_n))

    @pl.when(zl > 0)
    def _():
        nxt.start()

    bias = jnp.sum(hgw, 0, keepdims=True)
    for r in range(lanes):
        sm_c[0, pl.ds(2 * small_rows + r, 1), :] = bias[:, r * 128:(r + 1) * 128]
    pad = sm_c.shape[1] - 2 * small_rows - lanes
    if pad:
        sm_c[0, pl.ds(2 * small_rows + lanes, pad), :] = jnp.zeros((pad, 128), F32)
    sm_core = sems.start(sm_c.at[0], sm_c.at[1], at_core())

    def corr(base, ref0, x_first):
        group = ny * nx * NC * tile
        for zz in range(zhh):
            start = base + zz * group
            made = dot(unf[:, start:start + group], lg_v[...], 0, 0).astype(BF)
            for yy in range(ny):
                for xx in range(nx):
                    for cc in range(NC):
                        at = ((yy * nx + xx) * NC + cc) * tile
                        a, b = (xx, yy) if x_first else (yy, xx)
                        row = (b * zhh + zz) * tile
                        ref0[cc, a, row:row + tile, :] = made[at:at + tile, :]

    corr(0, ca_0, True)
    ca_core = sems.start(ca_0.at[1 - c], ca_c, at_core())
    pr_x = stage1(pr_core, pr_0, pr_c, pr_1, pr_r1, at_x, nx, x)
    corr(half, cb_0, False)
    cb_core = sems.start(cb_0.at[1 - c], cb_c, at_core())

    def small(copies, ref, me, n, nxt_ref):
        for copy in copies:
            copy.wait_recv()
        made = None
        for j in range(n):
            piece = ref[(me - j + n) % n]
            made = piece if made is None else made + piece
        nxt_ref[...] = made

    def small_send(ref, ring, n):
        return sems.ring(n, lambda d: ref.at[0], lambda d: ref.at[d], ring)

    small([sm_core], sm_c, c, NC, sm_x.at[0])
    sm_xs = small_send(sm_x, at_x, nx)

    s0_y = stage2(s0_x, s0_1, s0_r1, s0_2, s0_r2, at_y, ny, y, x)
    s1_x = stage2(s1_y, s1_1, s1_r1, s1_2, s1_r2, at_x, nx, x, y)
    pr_y = stage2(pr_x, pr_1, pr_r1, pr_2, pr_r2, at_y, ny, y, x)
    small(sm_xs, sm_x, x, nx, sm_y.at[0])
    sm_ys = small_send(sm_y, at_y, ny)
    ca_x = stage1(ca_core, ca_0, ca_c, ca_1, ca_r1, at_x, nx, x)
    cb_y = stage1(cb_core, cb_0, cb_c, cb_1, cb_r1, at_y, ny, y)

    @pl.when(zl == zl_n - 1)
    def _():
        next_v[...] = jnp.zeros(next_v.shape, BF)

    @pl.when(zl < zl_n - 1)
    def _():
        nxt.wait_recv()

    hgf[pl.ds(frames, 8), :] = next_v[...].astype(F32)[0:8, :]
    lg_next = hgf[pl.ds(1, frames), :].astype(BF)

    def feat_part(part):
        made = (dot(lg_next, cw_v[pl.ds(part * chan, chan), :], 1, 1)
                + dot(hid[...], cw_v[pl.ds(half + part * chan, chan), :], 1, 1))
        for k in range(lanes):
            fg_f[k, pl.ds(part, frames, stride=2), :] = made[:, k * 128:(k + 1) * 128]

    feat_part(0)

    s0_d = finish(s0_y, s0_2, s0_r2, y)
    s1_d = finish(s1_x, s1_2, s1_r2, x)
    pr_d = finish(pr_y, pr_2, pr_r2, y)
    for q in range(zl_n):
        zl_s[q] = jnp.concatenate(
            [s0_d[q * rs:(q + 1) * rs], s1_d[q * rs:(q + 1) * rs], pr_d], 0).astype(BF)
    zl_c = sems.ring(zl_n, lambda d: zl_s.at[(zl + d) % zl_n], lambda d: zl_r.at[d], at_l)
    zl_r[0] = zl_s[zl]
    small(sm_ys, sm_y, y, ny, sm_t)
    q_rows = per_q // 128
    for q in range(zl_n):
        for level in range(2):
            at = level * small_rows + q * q_rows
            sm_q[q, level * q_rows:(level + 1) * q_rows, :] = sm_t[at:at + q_rows, :]
        sm_q[q, 2 * q_rows:2 * q_rows + lanes, :] = sm_t[2 * small_rows:2 * small_rows + lanes, :]
        rest = sm_q.shape[1] - 2 * q_rows - lanes
        if rest:
            sm_q[q, 2 * q_rows + lanes:, :] = jnp.zeros((rest, 128), F32)
    sm_ls = [sems.start(sm_q.at[(zl + d) % zl_n], sm_l.at[d], at_l(d)) for d in range(1, zl_n)]
    sm_l[0] = sm_q[zl]

    def summed(copies, ref, me, n):
        for copy in copies:
            copy.wait_recv()
        made = None
        for j in range(n):
            piece = ref[(me - j + n) % n].astype(F32)
            made = piece if made is None else made + piece
        return made


    told(2)
    zh_r[0] = summed(zl_c, zl_r, zl, zl_n).astype(BF)
    zh_c = sems.ring(zh_n, lambda d: zh_r.at[0], lambda d: zh_r.at[d], at_h)
    small(sm_ls, sm_l, zl, zl_n, sm_h.at[0])
    sm_hs = small_send(sm_h, at_h, zh_n)

    ca_y = stage2(ca_x, ca_1, ca_r1, ca_2, ca_r2, at_y, ny, y, x)
    cb_x = stage2(cb_y, cb_1, cb_r1, cb_2, cb_r2, at_x, nx, x, y)

    ca_d = finish(ca_y, ca_2, ca_r2, y)
    cb_d = finish(cb_x, cb_2, cb_r2, x)
    for zz in range(zhh):
        ch_s[zz] = ca_d[zz * tile:(zz + 1) * tile].astype(BF)
        ch_s[zhh + zz] = cb_d[zz * tile:(zz + 1) * tile].astype(BF)
    ch_c = sems.ring(zh_n, lambda d: ch_s.at[(zh + d) % zh_n], lambda d: ch_r.at[d], at_h)
    ch_r[0] = ch_s[zh]

    feat_part(1)
    for k in range(lanes):
        fg_out[:, k * 128:(k + 1) * 128] = fg_f[k].astype(BF)

    small(sm_hs, sm_h, zh, zh_n, sm_f)
    base = c * per_c + (x * ny + y) * rs
    ids = lax.broadcasted_iota(jnp.int32, (rs, 128), 1) - lax.broadcasted_iota(jnp.int32, (rs, 128), 0)
    columns = []
    for level in range(2):
        row = sm_f[pl.ds(level * q_rows + base // 128, 1), :]
        columns.append(jnp.sum(jnp.where(ids == base % 128, row, 0.0), 1, keepdims=True))
    counts = jnp.maximum(jnp.concatenate(columns, 0), 1.0)

    done = summed(zh_c, zh_r, zh, zh_n)
    ag[c, x, y] = jnp.concatenate([done[:2 * rs] / counts, done[2 * rs:]], 0).astype(BF)
    steps = [(dx, dy) for dx in range(nx) for dy in range(ny) if dx or dy]
    steps.sort(key=lambda s: -(min(s[0], nx - s[0]) + min(s[1], ny - s[1])))
    plane = {
        (dx, dy): sems.start(ag.at[c, x, y], ag.at[c, x, y], dev(c, (x + dx) % nx, (y + dy) % ny, zh, zl))
        for dx, dy in steps
    }

    cl_r[0] = summed(ch_c, ch_r, zh, zh_n).astype(BF)
    cl_c = [sems.start(cl_r.at[0], cl_r.at[d], at_l(d)) for d in range(1, zl_n)]

    rows_in_order = sorted(range(nx), key=lambda d: min(d, nx - d))
    others = []
    for dx in rows_in_order:
        j = (x - dx + nx) % nx
        for dy in range(ny):
            if dx or dy:
                sems.arrived(plane[dx, dy], ag.at[c, j, (y - dy + ny) % ny], at_core())
        others.append((j, sems.start(ag.at[c, j], ag.at[c, j], at_core())))

    owned = summed(cl_c, cl_r, zl, zl_n)
    top = owned.astype(BF)
    low = (owned - top.astype(F32)).astype(BF)
    conv_f[...] = (dot(top, pw_v[...], 1, 1) + dot(low, pw_v[...], 1, 1)) / total
    for j, copy in others:
        sems.arrived(copy, ag.at[1 - c, j], at_core())

    for copy in sems.started:
        copy.wait_send()

    @pl.when(zl < zl_n - 1)
    def _():
        halo.wait_send()

    @pl.when(zl > 0)
    def _():
        nxt.wait_send()


def assemble(g, fg_in, conv_f, sm_f, ag, fg_out, conv_out, bias_out, proj_out, means_out, usage_out):
    nx, ny, zl_n, book, total = g["nx"], g["ny"], g["zl"], g["book"], g["total"]
    rs, rp, rpd, lanes = g["rs"], g["rp"], g["rpd"], g["chan"] // 128
    zl = lax.axis_index("tm")
    fg_out[...] = fg_in[...]
    picked = None
    for q in range(zl_n):
        piece = jnp.where(zl == q, conv_f[q * rpd:(q + 1) * rpd, :], 0.0)
        picked = piece if picked is None else picked + piece
    conv_out[...] = picked
    small_rows = book // 128
    q_rows = small_rows // zl_n
    per_c = nx * ny * rs
    for level in range(2):
        for r in range(q_rows):
            count = sm_f[level * q_rows + r:level * q_rows + r + 1, :]
            usage_out[level:level + 1, r * 128:(r + 1) * 128] = count * (book / total)
    for r in range(lanes):
        bias_out[:, r * 128:(r + 1) * 128] = sm_f[2 * q_rows + r:2 * q_rows + r + 1, :] / total
    for cc in range(NC):
        for xx in range(nx):
            for level in range(2):
                rows = [ag[cc, xx, yy].astype(F32)[level * rs:(level + 1) * rs] for yy in range(ny)]
                at = cc * per_c + xx * ny * rs
                means_out[level, at:at + ny * rs, :] = jnp.concatenate(rows, 0).astype(BF)
            for yy in range(ny):
                at = ((cc * nx + xx) * ny + yy) * rp
                proj_out[at:at + rp, :] = ag[cc, xx, yy].astype(F32)[2 * rs:] * (1.0 / total)


def shards(g, feats, codes, conv_weight, conv_bias, proj_weight, codebooks):
    rows_in, chan = feats.shape
    frames = rows_in // 2
    dz = proj_weight.shape[1]
    book = codebooks.shape[1]
    nx, ny, zhn, zln = g["nx"], g["ny"], g["zh"], g["zl"]
    devices = NC * nx * ny * zhn * zln
    taps = conv_weight.shape[0]
    g = dict(g, frames=frames, chan=chan, dz=dz, book=book, total=float(frames * devices),
             rs=book // (NC * nx * ny * zln), rp=chan // (NC * nx * ny), rpd=taps // devices)
    rs, rp, rpd = g["rs"], g["rp"], g["rpd"]
    tile = zln * rpd
    lanes = chan // 128

    def flow(a, b, rows):
        return [
            pltpu.VMEM((NC, a, b * rows, dz), BF),
            pltpu.VMEM((a, b * rows, dz), BF),
            pltpu.VMEM((a, b * rows, dz), BF),
            pltpu.VMEM((max(a - 1, 1), b * rows, dz), BF),
            pltpu.VMEM((b, rows, dz), BF),
            pltpu.VMEM((max(b - 1, 1), rows, dz), BF),
        ]

    small = -(-(2 * book // 128 + lanes) // 8) * 8
    few = -(-(2 * book // zln // 128 + lanes) // 8) * 8
    zrows = 2 * rs + rp
    scratch = [
        pltpu.VMEM((rows_in, chan), BF),
        pltpu.VMEM((1, 2, frames), jnp.int32),
        pltpu.VMEM((taps, chan), BF),
        pltpu.VMEM((1, chan), F32),
        pltpu.VMEM((chan, dz), BF),
        pltpu.VMEM((2, book, dz), BF),
        pltpu.VMEM((2, frames, book), BF),
        pltpu.VMEM((2, NC, book // NC, frames), BF),
        pltpu.VMEM((lanes, rows_in + 8, 128), F32),
        pltpu.VMEM((frames, taps), BF),
        pltpu.VMEM((frames, chan), F32),
        pltpu.VMEM((frames, chan), BF),
        pltpu.VMEM((frames, dz), F32),
        pltpu.VMEM((frames, dz), BF),
        pltpu.VMEM((frames + 8, chan), F32),
        pltpu.VMEM((16, chan), BF),
        pltpu.VMEM((16, chan), BF),
        pltpu.VMEM((lanes, rows_in, 128), F32),
    ]
    scratch += flow(nx, ny, zln * rs)
    scratch += flow(ny, nx, zln * rs)
    scratch += flow(nx, ny, rp)
    scratch += flow(nx, ny, zhn // 2 * tile)
    scratch += flow(ny, nx, zhn // 2 * tile)
    scratch += [pltpu.VMEM((n, small, 128), F32) for n in (NC, nx, ny)] + [pltpu.VMEM((small, 128), F32)]
    scratch += [pltpu.VMEM((n, few, 128), F32) for n in (zln, zln, zhn)]
    scratch += [
        pltpu.VMEM((zln, zrows, dz), BF),
        pltpu.VMEM((zln, zrows, dz), BF),
        pltpu.VMEM((zhn, zrows, dz), BF),
        pltpu.VMEM((zhn, tile, dz), BF),
        pltpu.VMEM((zhn, tile, dz), BF),
        pltpu.VMEM((zln, tile, dz), BF),
        pltpu.SemaphoreType.DMA((7,)),
        pltpu.SemaphoreType.REGULAR((3,)),
        pltpu.SemaphoreType.DMA((96,)),
        pltpu.SemaphoreType.DMA((96,)),
    ]
    hbm = pl.BlockSpec(memory_space=pltpu.HBM)
    vmem = pl.BlockSpec(memory_space=pltpu.VMEM)
    fg, conv_f, sm_f, ag = pl.pallas_call(
        functools.partial(kernel, g),
        out_shape=(
            pltpu.VMEM((rows_in, chan), BF),
            pltpu.VMEM((tile, chan), F32),
            pltpu.VMEM((few, 128), F32),
            pltpu.VMEM((NC, nx, ny, zrows, dz), BF),
        ),
        in_specs=[hbm] * 6,
        out_specs=(vmem,) * 4,
        scratch_shapes=scratch,
        compiler_params=pltpu.CompilerParams(
            collective_id=0, has_side_effects=True, vmem_limit_bytes=32 << 20),
    )(*[pltpu.with_memory_space_constraint(v, pltpu.HBM) for v in (
        feats, codes, conv_weight, conv_bias.reshape(1, chan), proj_weight, codebooks)])
    fg, cg, bg, pg, cm, cu = pl.pallas_call(
        functools.partial(assemble, g),
        out_shape=(
            jax.ShapeDtypeStruct((rows_in, chan), BF),
            jax.ShapeDtypeStruct((rpd, chan), F32),
            jax.ShapeDtypeStruct((1, chan), F32),
            jax.ShapeDtypeStruct((chan, dz), F32),
            jax.ShapeDtypeStruct((2, book // zln, dz), BF),
            jax.ShapeDtypeStruct((2, book // zln), F32),
        ),
        in_specs=[vmem] * 4,
        out_specs=(vmem, vmem, vmem, vmem, vmem, vmem),
        compiler_params=pltpu.CompilerParams(vmem_limit_bytes=8 << 20),
    )(fg, conv_f, sm_f, ag)
    return fg, cg, bg.reshape(chan), pg, cm, cu


def solution(mesh, g=None):
    if g is None:
        g = {"nx": 4, "ny": 4, "zh": 4, "zl": 4}
    placed = (P(("dp", "tm"), None), P("dp", None, "tm"), P(), P(), P(), P())
    return jax.shard_map(
        functools.partial(shards, g),
        mesh=mesh,
        in_specs=placed,
        out_specs=(
            P(("dp", "tm"), None),
            P(("dp", "tm"), None),
            P(),
            P(),
            P(None, "tm", None),
            P(None, "tm"),
        ),
        check_vma=False,
    )
```
